512 devices in a mesh: section: 16 (over z), expert: 8 (over y, core), dp: 4 (over x).
Axes of the slice: x: 4, y: 4, z: 16, core: 2. Of those that a mesh axis runs over, the one named last changes fastest.
Arguments:
- tokens: bfloat16 [1024, 3072], P('expert', 'dp'), may hold values from -6 to 6
- expert_ids: int32 [1024, 2], P('expert'), may hold values from 0 to 7, all different within a row; in each aligned block of 128 rows (0 to 127, 128 to 255, ...) at most 64 rows name the same one
- w_gate: bfloat16 [8, 3072, 8192], P('expert', 'dp', 'section'), may hold values from -0.109375 to 0.109375
- w_up: bfloat16 [8, 3072, 8192], P('expert', 'dp', 'section'), may hold values from -0.109375 to 0.109375
- cotangent: bfloat16 [8, 512, 8192], P('expert', None, 'section'), may hold values from -6 to 6
Outputs:
- acted: bfloat16 [8, 512, 8192], P('expert', None, 'section')
- input_grad: bfloat16 [1024, 3072], P('expert', 'dp')
- gate_grad: bfloat16 [8, 3072, 8192], P('expert', 'dp', 'section')
- up_grad: bfloat16 [8, 3072, 8192], P('expert', 'dp', 'section')
The draws below stay inside these ranges and needn't reach their ends.
Inputs may be any that keep to these rules, and one draw needn't show every extreme that they name: `expert_ids`: each token names two different experts. Among the 128 tokens of one index of the expert axis no expert is named more than 64 times, a bound that some block reaches.
All inputs are finite; a program needn't handle non-finite values.
Results may differ from the reference program's by a relative error of at most 0.0049.
Values may be sent and summed in bfloat16 or wider, within the bound.
A program may use at most 64 MiB of HBM per device.

```python
import math
import jax
import jax.numpy as jnp
import numpy as np
from jax import lax

D = 3072
FF = 8192
TOK_DEV = 128
EXPERTS = 8
TOKENS = 1024
CAP = 64
SLOTS = 512
N_EXPERT = 8


def level_of(key, shape, pieces, least, largest):
    loudness, own = 1.0, jax.random.fold_in(key, 6)
    for dim, parts in pieces:
        heights = jnp.exp(jax.random.uniform(jax.random.fold_in(own, dim), (parts,), jnp.float32, least / len(pieces), largest / len(pieces)))
        loudness = loudness * jnp.repeat(heights, shape[dim] // parts).reshape([-1 if axis == dim else 1 for axis in range(len(shape))])
    return loudness


def deal_out(rng, own, number, rows, count, top, limit, slope):
    ranking = jax.random.permutation(rng, count)
    heavy_load, common = shares(count, rows * top, limit, slope, True), shares(count, rows * top, limit, slope, False)
    places = jnp.arange(count)

    def named(lengths, offset_by):
        used = int((lengths > 0).sum())
        fixed = max(1, used // 4)
        passed = fixed + (places - fixed + offset_by * (used - fixed)) % max(1, count - fixed)
        return jnp.zeros((count,), jnp.int32).at[ranking[jnp.where(places < fixed, places, passed)]].set(jnp.asarray(lengths, jnp.int32))

    lengths = jnp.where(number % 4 == 0, named(heavy_load, number // 4), named(common, number - number // 4 - 1))
    mixed = jax.random.permutation(jax.random.fold_in(own, 3), count)
    source_of, receiver = mixed[0:count // 2 * 2:2], mixed[1:count // 2 * 2:2]
    margin = jnp.minimum(lengths[source_of] - 1, limit - lengths[receiver]) // 2
    margin = jnp.where((source_of == ranking[0]) | (receiver == ranking[0]) | (lengths[receiver] == 0), 0, jnp.maximum(margin, 0))
    passed = jax.random.randint(jax.random.fold_in(own, 4), (count // 2,), 0, 1 << 20) % (margin + 1)
    lengths = lengths.at[source_of].add(-passed).at[receiver].add(passed)
    items = jnp.searchsorted(jnp.cumsum(lengths), jnp.arange(rows * top), side="right").astype(jnp.int32)
    table = items.reshape(top, rows).T
    table = table[jax.random.permutation(jax.random.fold_in(own, 1), rows)]
    offset_by = jax.random.randint(jax.random.fold_in(own, 2), (rows, 1), 0, top)
    return jnp.take_along_axis(table, (jnp.arange(top)[None, :] + offset_by) % top, axis=1)


def shares(count, total, most, skew, full):
    loads = [(1 << 20) // math.isqrt(grade ** skew) + 1 for grade in range(1, count + 1)]
    largest = most if full else min(most, max(-(-total // count), total * loads[0] // sum(loads)))
    least = 1 if total - largest >= count - 1 else 0
    counts, rest = [largest] + [least] * (count - 1), total - largest - least * (count - 1)
    while rest > 0:
        movable = [i for i in range(1, count) if counts[i] < largest] or [i for i in range(1, count) if counts[i] < most]
        pool, left = sum([loads[i] for i in movable]), rest
        for i in movable:
            addition = min(most - counts[i], max(1, left * loads[i] // pool), rest)
            counts[i] = counts[i] + addition
            rest = rest - addition
    return np.array(counts)


def centred(own_key, extent, scale, most, cuts=(), kind=jnp.bfloat16):
    result = jax.random.normal(own_key, extent, jnp.float32) * scale
    if len(cuts) > 0:
        result = level_of(own_key, extent, cuts, -0.22, 0.18) * result
    return jnp.clip(result, min=-most, max=most).astype(kind)


def setup_inputs(seed: int = 0) -> dict:
    streams_of = jax.random.split(jax.random.key(seed), 6)
    tokens = centred(streams_of[0], (TOKENS, D), 1.0, 6.0, ((0, 8), (1, 4)))
    expert_ids_keys = jax.random.split(jax.random.fold_in(streams_of[1], 1), TOKENS // TOK_DEV)
    expert_ids_turns = jax.random.permutation(jax.random.fold_in(streams_of[1], 3), TOKENS // TOK_DEV)
    expert_ids = jax.vmap(lambda own, number: deal_out(jax.random.fold_in(streams_of[1], 2), own, number, TOK_DEV, EXPERTS, 2, CAP, 2))(expert_ids_keys, expert_ids_turns).reshape((TOKENS, 2))
    w_gate = centred(streams_of[2], (EXPERTS, D, FF), D ** -0.5, 0.109375, ((0, 8), (1, 4), (2, 16)))
    w_up = centred(streams_of[3], (EXPERTS, D, FF), D ** -0.5, 0.109375, ((0, 8), (1, 4), (2, 16)))
    cotangent = centred(streams_of[4], (EXPERTS, SLOTS, FF), 1.0, 6.0, ((0, 8), (2, 16)))
    return dict(tokens=tokens, expert_ids=expert_ids, w_gate=w_gate, w_up=w_up, cotangent=cotangent)


def expert_slots(ids, which):
    hits = (ids == which).reshape(N_EXPERT, 2 * TOK_DEV).astype(jnp.int32)
    rank = jnp.cumsum(hits, axis=1) - hits
    group = jnp.arange(N_EXPERT, dtype=jnp.int32)[:, None]
    slot = jnp.where(hits > 0, group * CAP + rank, N_EXPERT * CAP).astype(jnp.int32)
    token = (jnp.arange(TOKENS * 2, dtype=jnp.int32) // 2).reshape(N_EXPERT, 2 * TOK_DEV)
    source = jnp.full((N_EXPERT * CAP,), TOKENS, jnp.int32).at[slot.reshape(-1)].set(
        token.reshape(-1), mode="drop")
    return slot.reshape(-1), source


def reference(tokens, expert_ids, w_gate, w_up, cotangent):
    x_pad = jnp.concatenate([tokens, jnp.zeros((1, D), jnp.bfloat16)], axis=0)

    def per_expert(carry, item):
        which, wg, wu, cot = item
        slot, source = expert_slots(expert_ids, which)
        rows = jnp.take(x_pad, source, axis=0)
        pre_gate = jnp.dot(rows, wg, preferred_element_type=jnp.float32)
        pre_up = jnp.dot(rows, wu, preferred_element_type=jnp.float32)
        sig = jax.nn.sigmoid(pre_gate)
        silu_v = pre_gate * sig
        acted = (silu_v * pre_up).astype(jnp.bfloat16)
        cf = cot.astype(jnp.float32)
        gate_part = (cf * pre_up * sig * (1.0 + pre_gate * (1.0 - sig))).astype(jnp.bfloat16)
        up_part = (cf * silu_v).astype(jnp.bfloat16)
        gate_grad = jnp.dot(rows.T, gate_part, preferred_element_type=jnp.float32).astype(jnp.bfloat16)
        up_grad = jnp.dot(rows.T, up_part, preferred_element_type=jnp.float32).astype(jnp.bfloat16)
        back = (jnp.dot(gate_part, wg.T, preferred_element_type=jnp.float32)
                + jnp.dot(up_part, wu.T, preferred_element_type=jnp.float32))
        back_pad = jnp.concatenate([back, jnp.zeros((1, D), jnp.float32)], axis=0)
        per_token = jnp.take(back_pad, slot, axis=0).reshape(TOKENS, 2, D)
        carry = carry + jnp.sum(per_token, axis=1)
        return carry, (acted, gate_grad, up_grad)

    numbers = jnp.arange(EXPERTS).astype(jnp.int32)
    start = jnp.zeros((TOKENS, D), jnp.float32)
    total, outs = lax.scan(per_expert, start, (numbers, w_gate, w_up, cotangent))
    return (outs[0], total.astype(jnp.bfloat16), outs[1], outs[2])
```

```python
import jax
import jax.numpy as jnp
from jax import lax
from jax.experimental import pallas as pl
from jax.experimental.pallas import tpu as pltpu
from jax.sharding import PartitionSpec as P

F32 = jnp.float32
BF16 = jnp.bfloat16
NN = (((1,), (0,)), ((), ()))
NT = (((1,), (1,)), ((), ()))
TN = (((0,), (0,)), ((), ()))


def dot(a, b, dims):
    return lax.dot_general(a, b, dims, preferred_element_type=F32)


def kernel(
    sizes,
    tok, slots, wg, wu, cot,
    acted, grad_in, grad_gate, grad_up,
    pick, x_out, x_all, pre_out, pre_in, pre_own, pre_all,
    gate_part, up_part, back_out, home, whole, z_out, z_in, z_all,
    x_ss, x_rs, p_ss, p_rs, a_ss, a_rs, h_ss, h_rs, zr_ss, zr_rs, za_ss, za_rs,
):
    ns, ne, nd = sizes
    s, e, d = lax.axis_index("section"), lax.axis_index("expert"), lax.axis_index("dp")
    cap = x_all.shape[0] // ne
    hid = wg.shape[1]
    per = ne // nd
    y, c = e // 2, e % 2
    ny = ne // 2

    def rows(g):
        return pl.ds(pl.multiple_of(g * cap, cap), cap)

    def expert_peer(k):
        return ((y + k // 2) % ny) * 2 + (c + k) % 2

    def send(src, dst, ss, rs, axis, peer):
        return pltpu.make_async_remote_copy(
            src_ref=src, dst_ref=dst, send_sem=ss, recv_sem=rs,
            device_id={axis: peer}, device_id_type=pl.DeviceIdType.MESH,
        )

    barrier = pltpu.get_barrier_semaphore()
    for axis, me, n in (("section", s, ns), ("expert", e, ne), ("dp", d, nd)):
        for k in range(1, n):
            pl.semaphore_signal(
                barrier, inc=1, device_id={axis: (me + k) % n},
                device_id_type=pl.DeviceIdType.MESH,
            )

    at = lax.broadcasted_iota(jnp.int32, pick.shape, 0)
    pick[...] = jnp.where(
        (at == slots[0:1, :]) | (at == slots[1:2, :]), 1.0, 0.0
    ).astype(BF16)

    def build(g, _):
        x_out[rows(g), :] = dot(pick[rows(g), :], tok[...], NN).astype(BF16)
        return 0

    lax.fori_loop(0, ne, build, 0)
    x_all[rows(e), :] = x_out[rows(e), :]
    pl.semaphore_wait(barrier, ns + ne + nd - 3)

    def x_copy(peer, slot):
        return send(
            x_out.at[rows(peer)], x_all.at[rows(slot)], x_ss.at[peer], x_rs.at[slot],
            "expert", peer,
        )

    for k in range(1, ne):
        x_copy(expert_peer(k), e).start()

    def p_copy(g):
        i = g // nd
        return send(
            pre_out.at[rows(g)], pre_in.at[i, d], p_ss.at[g], p_rs.at[i, d], "dp", g % nd
        )

    def forward(k, _):
        g = expert_peer(k)

        @pl.when(k > 0)
        def _():
            x_copy(g, g).wait_recv()

        x = x_all[rows(g), :]
        pg = dot(x, wg[...], NN)
        pu = dot(x, wu[...], NN)

        @pl.when(g % nd == d)
        def _():
            pre_own[g // nd, :, :hid] = pg
            pre_own[g // nd, :, hid:] = pu

        @pl.when(g % nd != d)
        def _():
            pre_out[rows(g), :hid] = pg.astype(BF16)
            pre_out[rows(g), hid:] = pu.astype(BF16)
            p_copy(g).start()

        return 0

    lax.fori_loop(0, ne, forward, 0)

    def a_copy(i, peer, g):
        return send(
            pre_all.at[rows(g)], pre_all.at[rows(g)], a_ss.at[i, peer], a_rs.at[g], "dp", peer
        )

    def owned(i, _):
        total = pre_own[i]
        for k in range(1, nd):
            src = (d + k) % nd
            send(
                pre_out.at[rows(0)], pre_in.at[i, src], p_ss.at[0], p_rs.at[i, src], "dp", src
            ).wait_recv()
            total = total + pre_in[i, src].astype(F32)
        g = i * nd + d
        pre_all[rows(g), :] = total.astype(BF16)
        for k in range(1, nd):
            a_copy(i, (d + k) % nd, g).start()
        return 0

    lax.fori_loop(0, per, owned, 0)

    def h_copy(g):
        return send(back_out.at[rows(g)], home.at[rows(e)], h_ss.at[g], h_rs.at[e], "expert", g)

    def backward(t, _):
        i, k = t // nd, t % nd
        src = (d + k) % nd
        g = i * nd + src

        @pl.when(k > 0)
        def _():
            a_copy(i, src, g).wait_recv()

        pre_gate = pre_all[rows(g), :hid].astype(F32)
        pre_up = pre_all[rows(g), hid:].astype(F32)
        cf = cot[rows(g), :].astype(F32)
        sig = jax.nn.sigmoid(pre_gate)
        silu = pre_gate * sig
        acted[rows(g), :] = (silu * pre_up).astype(BF16)
        gp = (cf * pre_up * sig * (1.0 + pre_gate * (1.0 - sig))).astype(BF16)
        up = (cf * silu).astype(BF16)
        gate_part[rows(g), :] = gp
        up_part[rows(g), :] = up
        back = (dot(gp, wg[...], NT) + dot(up, wu[...], NT)).astype(BF16)

        @pl.when(g == e)
        def _():
            home[rows(g), :] = back

        @pl.when(g != e)
        def _():
            back_out[rows(g), :] = back
            h_copy(g).start()

        return 0

    lax.fori_loop(0, ne, backward, 0)

    tile = 128

    def weights(i, _):
        at = pl.ds(pl.multiple_of(i * tile, tile), tile)
        x = x_all[:, at]
        grad_gate[at, :] = dot(x, gate_part[...], TN).astype(BF16)
        grad_up[at, :] = dot(x, up_part[...], TN).astype(BF16)
        return 0

    lax.fori_loop(0, wg.shape[0] // tile, weights, 0)

    for k in range(1, ne):
        src = expert_peer(k)
        send(
            back_out.at[rows(src)], home.at[rows(src)], h_ss.at[src], h_rs.at[src], "expert", src
        ).wait_recv()
    part = dot(pick[...], home[...], TN).reshape(whole.shape)
    whole[...] = part
    z_out[...] = part.astype(BF16)

    far = [k for j in range(ns // 2, 0, -1) for k in dict.fromkeys((j, ns - j))]

    def zr_copy(peer, slot):
        return send(
            z_out.at[peer], z_in.at[slot], zr_ss.at[peer], zr_rs.at[slot], "section", peer
        )

    def za_copy(peer, slot):
        return send(
            z_all.at[slot], z_all.at[slot], za_ss.at[peer], za_rs.at[slot], "section", peer
        )

    for k in far:
        zr_copy((s + k) % ns, s).start()
    total = whole[s]
    for k in reversed(far):
        src = (s + k) % ns
        zr_copy(src, src).wait_recv()
        total = total + z_in[src].astype(F32)
    z_all[s] = total.astype(BF16)
    for k in far:
        za_copy((s + k) % ns, s).start()
    for k in reversed(far):
        src = (s + k) % ns
        za_copy(src, src).wait_recv()
    grad_in[...] = z_all[...]

    for k in range(1, ne):
        x_copy(expert_peer(k), e).wait_send()
        h_copy(expert_peer(k)).wait_send()
    for i in range(per):
        for k in range(1, nd):
            p_copy(i * nd + (d + k) % nd).wait_send()
            a_copy(i, (d + k) % nd, i * nd + d).wait_send()
    for k in far:
        zr_copy((s + k) % ns, s).wait_send()
        za_copy((s + k) % ns, s).wait_send()


def local(tokens, expert_ids, w_gate, w_up, cotangent):
    count, width = tokens.shape
    ns, ne, nd = (lax.axis_size(a) for a in ("section", "expert", "dp"))
    hid = w_gate.shape[2]
    slots = cotangent.shape[1]
    cap = slots // ne
    flat = expert_ids.reshape(-1)
    order = jnp.arange(2 * count, dtype=jnp.int32)
    earlier = (flat[:, None] == flat[None, :]) & (order[None, :] < order[:, None])
    slot = flat * cap + jnp.sum(earlier.astype(jnp.int32), axis=1)
    slot = slot.reshape(count, 2).T

    vmem = pl.BlockSpec(memory_space=pltpu.VMEM)
    dma = pltpu.SemaphoreType.DMA
    share = count // ns
    acted, grad_in, grad_gate, grad_up = pl.pallas_call(
        lambda *refs: kernel((ns, ne, nd), *refs),
        out_shape=(
            jax.ShapeDtypeStruct((slots, hid), BF16),
            jax.ShapeDtypeStruct((ns, share, width), BF16),
            jax.ShapeDtypeStruct((width, hid), BF16),
            jax.ShapeDtypeStruct((width, hid), BF16),
        ),
        in_specs=[vmem] * 5,
        out_specs=(vmem,) * 4,
        scratch_shapes=[
            pltpu.VMEM((slots, count), BF16),
            pltpu.VMEM((slots, width), BF16),
            pltpu.VMEM((slots, width), BF16),
            pltpu.VMEM((slots, 2 * hid), BF16),
            pltpu.VMEM((ne // nd, nd, cap, 2 * hid), BF16),
            pltpu.VMEM((ne // nd, cap, 2 * hid), F32),
            pltpu.VMEM((slots, 2 * hid), BF16),
            pltpu.VMEM((slots, hid), BF16),
            pltpu.VMEM((slots, hid), BF16),
            pltpu.VMEM((slots, width), BF16),
            pltpu.VMEM((slots, width), BF16),
            pltpu.VMEM((ns, share, width), F32),
            pltpu.VMEM((ns, share, width), BF16),
            pltpu.VMEM((ns, share, width), BF16),
            pltpu.VMEM((ns, share, width), BF16),
            dma((ne,)), dma((ne,)),
            dma((ne,)), dma((ne // nd, nd)),
            dma((ne // nd, nd)), dma((ne,)),
            dma((ne,)), dma((ne,)),
            dma((ns,)), dma((ns,)),
            dma((ns,)), dma((ns,)),
        ],
        compiler_params=pltpu.CompilerParams(collective_id=0, has_side_effects=True),
    )(tokens, slot, w_gate[0], w_up[0], cotangent[0])
    return acted[None], grad_in.reshape(count, width), grad_gate[None], grad_up[None]


def solution(mesh):
    placed = (
        P("expert", "dp"),
        P("expert", None),
        P("expert", "dp", "section"),
        P("expert", "dp", "section"),
        P("expert", None, "section"),
    )
    return jax.shard_map(
        local,
        mesh=mesh,
        in_specs=placed,
        out_specs=(
            P("expert", None, "section"),
            P("expert", "dp"),
            P("expert", "dp", "section"),
            P("expert", "dp", "section"),
        ),
        check_vma=False,
    )
```

```python
import jax
import jax.numpy as jnp
from jax import lax
from jax.experimental import pallas as pl
from jax.experimental.pallas import tpu as pltpu
from jax.sharding import PartitionSpec as P

F32 = jnp.float32
BF16 = jnp.bfloat16
NN = (((1,), (0,)), ((), ()))
NT = (((1,), (1,)), ((), ()))
TN = (((0,), (0,)), ((), ()))


def dot(a, b, dims):
    return lax.dot_general(a, b, dims, preferred_element_type=F32)


def kernel(
    sizes,
    tok, ids, wg_hbm, wu_hbm, cot_hbm,
    acted_hbm, grad_in, gate_hbm, up_hbm,
    wg, wu, cot, acted, grad_gate, grad_up,
    pick, x_out, x_all, pre_out, pre_in, pre_own, parts,
    back_out, home, whole, z_out, z_in, z_all,
    in_sem, out_sem,
    x_ss, x_rs, p_ss, p_rs, a_ss, a_rs, o_ss, o_rs, h_ss, h_rs, zr_ss, zr_rs, za_ss, za_rs,
):
    ns, ne, nd = sizes
    s, e, d = lax.axis_index("section"), lax.axis_index("expert"), lax.axis_index("dp")
    cap = x_all.shape[0] // ne
    hid = wg.shape[1]
    per = ne // nd
    y, c = e // 2, e % 2
    ny = ne // 2

    def rows(g):
        return pl.ds(pl.multiple_of(g * cap, cap), cap)

    def expert_peer(k):
        return ((y + k // 2) % ny) * 2 + (c + k) % 2

    def send(src, dst, ss, rs, axis, peer):
        return pltpu.make_async_remote_copy(
            src_ref=src, dst_ref=dst, send_sem=ss, recv_sem=rs,
            device_id={axis: peer}, device_id_type=pl.DeviceIdType.MESH,
        )

    barrier = pltpu.get_barrier_semaphore()
    for axis, me, n in (("section", s, ns), ("expert", e, ne), ("dp", d, nd)):
        for k in range(1, n):
            pl.semaphore_signal(
                barrier, inc=1, device_id={axis: (me + k) % n},
                device_id_type=pl.DeviceIdType.MESH,
            )

    loads = [
        pltpu.make_async_copy(src, dst, in_sem.at[i])
        for i, (src, dst) in enumerate(((wg_hbm, wg), (wu_hbm, wu), (cot_hbm, cot)))
    ]
    for copy in loads:
        copy.start()

    count = tok.shape[0]
    named = lax.broadcasted_iota(jnp.int32, (ne, count), 0)
    member = (named == ids[0:1, :]) | (named == ids[1:2, :])
    before = lax.broadcasted_iota(jnp.int32, (count, count), 0) < lax.broadcasted_iota(
        jnp.int32, (count, count), 1
    )
    rank = dot(
        jnp.where(member, 1.0, 0.0).astype(BF16), jnp.where(before, 1.0, 0.0).astype(BF16), NN
    ).astype(jnp.int32)
    rank = jnp.where(member, rank, -1)
    at = lax.broadcasted_iota(jnp.int32, (cap, count), 0)
    for g in range(ne):
        pick[g * cap : (g + 1) * cap, :] = jnp.where(at == rank[g : g + 1, :], 1.0, 0.0).astype(
            BF16
        )

    def build(g, _):
        x_out[rows(g), :] = dot(pick[rows(g), :], tok[...], NN).astype(BF16)
        return 0

    lax.fori_loop(0, ne, build, 0)
    x_all[rows(e), :] = x_out[rows(e), :]
    pl.semaphore_wait(barrier, ns + ne + nd - 3)

    def x_copy(peer, slot):
        return send(
            x_out.at[rows(peer)], x_all.at[rows(slot)], x_ss.at[peer], x_rs.at[slot],
            "expert", peer,
        )

    for k in range(1, ne):
        x_copy(expert_peer(k), e).start()

    def p_copy(g):
        i = g // nd
        return send(
            pre_out.at[rows(g)], pre_in.at[i, d], p_ss.at[g], p_rs.at[i, d], "dp", g % nd
        )

    for copy in loads[:2]:
        copy.wait()

    def forward(t, _):
        k = jnp.where(t < 4, t, jnp.where(t < 6, t + 2, t - 2))
        g = expert_peer(k)

        @pl.when(t > 0)
        def _():
            x_copy(g, g).wait_recv()

        x = x_all[rows(g), :]
        pg = dot(x, wg[...], NN)
        pu = dot(x, wu[...], NN)

        @pl.when(g % nd == d)
        def _():
            pre_own[g // nd, :, :hid] = pg
            pre_own[g // nd, :, hid:] = pu

        @pl.when(g % nd != d)
        def _():
            pre_out[rows(g), :hid] = pg.astype(BF16)
            pre_out[rows(g), hid:] = pu.astype(BF16)
            p_copy(g).start()

        return 0

    lax.fori_loop(0, ne, forward, 0)

    def a_copy(peer, g):
        return send(
            parts.at[rows(g)], parts.at[rows(g)], a_ss.at[g // nd, peer], a_rs.at[g], "dp", peer
        )

    def o_copy(peer, g):
        return send(
            acted.at[rows(g)], acted.at[rows(g)], o_ss.at[g // nd, peer], o_rs.at[g], "dp", peer
        )

    loads[2].wait()
    first = y // (ny // per)

    def owned(t, _):
        i = (first + t) % per
        total = pre_own[i]
        for k in range(1, nd):
            src = (d + k) % nd
            send(
                pre_out.at[rows(0)], pre_in.at[i, src], p_ss.at[0], p_rs.at[i, src], "dp", src
            ).wait_recv()
            total = total + pre_in[i, src].astype(F32)
        g = i * nd + d
        pre_gate, pre_up = total[:, :hid], total[:, hid:]
        cf = cot[rows(g), :].astype(F32)
        sig = jax.nn.sigmoid(pre_gate)
        silu = pre_gate * sig
        gp = cf * pre_up * sig * (1.0 + pre_gate * (1.0 - sig))
        parts[rows(g), :hid] = gp.astype(BF16)
        parts[rows(g), hid:] = (cf * silu).astype(BF16)
        acted[rows(g), :] = (silu * pre_up).astype(BF16)
        for k in range(1, nd):
            a_copy((d + k) % nd, g).start()
        return 0

    lax.fori_loop(0, per, owned, 0)
    for i in range(per):
        for k in range(1, nd):
            o_copy((d + k) % nd, i * nd + d).start()

    def h_copy(g):
        return send(back_out.at[rows(g)], home.at[rows(e)], h_ss.at[g], h_rs.at[e], "expert", g)

    def backward(t, _):
        k = t % nd
        src = (d + k) % nd
        g = (first + t // nd) % per * nd + src

        @pl.when(k > 0)
        def _():
            a_copy(src, g).wait_recv()

        back = dot(parts[rows(g), :hid], wg[...], NT) + dot(parts[rows(g), hid:], wu[...], NT)

        @pl.when(g == e)
        def _():
            home[rows(g), :] = back.astype(BF16)

        @pl.when(g != e)
        def _():
            back_out[rows(g), :] = back.astype(BF16)
            h_copy(g).start()

        return 0

    lax.fori_loop(0, ne, backward, 0)

    tile = 128

    def weights(i, _):
        at = pl.ds(pl.multiple_of(i * tile, tile), tile)
        x = x_all[:, at]
        grad_gate[at, :] = dot(x, parts[:, :hid], TN).astype(BF16)
        grad_up[at, :] = dot(x, parts[:, hid:], TN).astype(BF16)
        return 0

    lax.fori_loop(0, wg.shape[0] // tile, weights, 0)
    stores = [
        pltpu.make_async_copy(src, dst, out_sem.at[i])
        for i, (src, dst) in enumerate(
            ((grad_gate, gate_hbm), (grad_up, up_hbm), (acted, acted_hbm))
        )
    ]
    for copy in stores[:2]:
        copy.start()

    for k in range(1, ne):
        src = expert_peer(k)
        send(
            back_out.at[rows(src)], home.at[rows(src)], h_ss.at[src], h_rs.at[src], "expert", src
        ).wait_recv()
    part = dot(pick[...], home[...], TN).reshape(whole.shape)
    whole[...] = part
    z_out[...] = part.astype(BF16)

    far = [k for j in range(ns // 2, 0, -1) for k in dict.fromkeys((j, ns - j))]

    def zr_copy(peer, slot):
        return send(
            z_out.at[peer], z_in.at[slot], zr_ss.at[peer], zr_rs.at[slot], "section", peer
        )

    def za_copy(peer, slot):
        return send(
            z_all.at[slot], z_all.at[slot], za_ss.at[peer], za_rs.at[slot], "section", peer
        )

    for k in far:
        zr_copy((s + k) % ns, s).start()
    total = whole[s]
    for k in reversed(far):
        src = (s + k) % ns
        zr_copy(src, src).wait_recv()
        total = total + z_in[src].astype(F32)
    z_all[s] = total.astype(BF16)
    for k in far:
        za_copy((s + k) % ns, s).start()
    for i in range(per):
        for k in range(1, nd):
            src = (d + k) % nd
            o_copy(src, i * nd + src).wait_recv()
    stores[2].start()
    for k in reversed(far):
        src = (s + k) % ns
        za_copy(src, src).wait_recv()
    grad_in[...] = z_all[...]

    for k in range(1, ne):
        x_copy(expert_peer(k), e).wait_send()
        h_copy(expert_peer(k)).wait_send()
    for i in range(per):
        for k in range(1, nd):
            p_copy(i * nd + (d + k) % nd).wait_send()
            a_copy((d + k) % nd, i * nd + d).wait_send()
            o_copy((d + k) % nd, i * nd + d).wait_send()
    for k in far:
        zr_copy((s + k) % ns, s).wait_send()
        za_copy((s + k) % ns, s).wait_send()
    for copy in stores:
        copy.wait()


def settle(*refs):
    n = (len(refs) - 2) // 3
    src, dst, held, (in_sem, out_sem) = refs[:n], refs[n : 2 * n], refs[2 * n : 3 * n], refs[3 * n :]
    reads = [pltpu.make_async_copy(src[i], held[i], in_sem.at[i]) for i in range(n)]
    writes = [pltpu.make_async_copy(held[i], dst[i], out_sem.at[i]) for i in range(n)]
    for copy in reads:
        copy.start()
    for i in range(n):
        reads[i].wait()
        writes[i].start()
    for copy in writes:
        copy.wait()


def local(tokens, expert_ids, w_gate, w_up, cotangent):
    count, width = tokens.shape
    ns, ne, nd = (lax.axis_size(a) for a in ("section", "expert", "dp"))
    hid = w_gate.shape[2]
    slots = cotangent.shape[1]
    cap = slots // ne
    vmem = pl.BlockSpec(memory_space=pltpu.VMEM)
    dma = pltpu.SemaphoreType.DMA
    share = count // ns
    anywhere = pl.BlockSpec(memory_space=pl.ANY)
    outs = pl.pallas_call(
        lambda *refs: kernel((ns, ne, nd), *refs),
        out_shape=(
            jax.ShapeDtypeStruct((slots, hid), BF16),
            jax.ShapeDtypeStruct((ns, share, width), BF16),
            jax.ShapeDtypeStruct((width, hid), BF16),
            jax.ShapeDtypeStruct((width, hid), BF16),
        ),
        in_specs=[vmem] * 2 + [anywhere] * 3,
        out_specs=(anywhere, vmem, anywhere, anywhere),
        scratch_shapes=[
            pltpu.VMEM((width, hid), BF16),
            pltpu.VMEM((width, hid), BF16),
            pltpu.VMEM((slots, hid), BF16),
            pltpu.VMEM((slots, hid), BF16),
            pltpu.VMEM((width, hid), BF16),
            pltpu.VMEM((width, hid), BF16),
            pltpu.VMEM((slots, count), BF16),
            pltpu.VMEM((slots, width), BF16),
            pltpu.VMEM((slots, width), BF16),
            pltpu.VMEM((slots, 2 * hid), BF16),
            pltpu.VMEM((ne // nd, nd, cap, 2 * hid), BF16),
            pltpu.VMEM((ne // nd, cap, 2 * hid), F32),
            pltpu.VMEM((slots, 2 * hid), BF16),
            pltpu.VMEM((slots, width), BF16),
            pltpu.VMEM((slots, width), BF16),
            pltpu.VMEM((ns, share, width), F32),
            pltpu.VMEM((ns, share, width), BF16),
            pltpu.VMEM((ns, share, width), BF16),
            pltpu.VMEM((ns, share, width), BF16),
            dma((3,)), dma((3,)),
            dma((ne,)), dma((ne,)),
            dma((ne,)), dma((ne // nd, nd)),
            dma((ne // nd, nd)), dma((ne,)),
            dma((ne // nd, nd)), dma((ne,)),
            dma((ne,)), dma((ne,)),
            dma((ns,)), dma((ns,)),
            dma((ns,)), dma((ns,)),
        ],
        compiler_params=pltpu.CompilerParams(collective_id=0, has_side_effects=True),
    )(tokens, expert_ids.T, w_gate[0], w_up[0], cotangent[0])
    n = len(outs)
    acted, grad_in, grad_gate, grad_up = pl.pallas_call(
        settle,
        out_shape=tuple(jax.ShapeDtypeStruct(o.shape, o.dtype) for o in outs),
        in_specs=[anywhere] * n,
        out_specs=(anywhere,) * n,
        scratch_shapes=[pltpu.VMEM(o.shape, o.dtype) for o in outs] + [dma((n,)), dma((n,))],
    )(*outs)
    return acted[None], grad_in.reshape(count, width), grad_gate[None], grad_up[None]


def solution(mesh):
    placed = (
        P("expert", "dp"),
        P("expert", None),
        P("expert", "dp", "section"),
        P("expert", "dp", "section"),
        P("expert", None, "section"),
    )
    return jax.shard_map(
        local,
        mesh=mesh,
        in_specs=placed,
        out_specs=(
            P("expert", None, "section"),
            P("expert", "dp"),
            P("expert", "dp", "section"),
            P("expert", "dp", "section"),
        ),
        check_vma=False,
    )
```

```python
import jax
import jax.numpy as jnp
from jax import lax
from jax.experimental import pallas as pl
from jax.experimental.pallas import tpu as pltpu
from jax.sharding import PartitionSpec as P

F32 = jnp.float32
BF16 = jnp.bfloat16
NN = (((1,), (0,)), ((), ()))
NT = (((1,), (1,)), ((), ()))
TN = (((0,), (0,)), ((), ()))


def dot(a, b, dims):
    return lax.dot_general(a, b, dims, preferred_element_type=F32)


def kernel(
    sizes,
    tok, ids, wg_hbm, wu_hbm, cot_hbm,
    acted_hbm, grad_in, gate_hbm, up_hbm,
    wg, wu, cot, acted, grad_gate, grad_up,
    pick, x_out, x_all, pre_out, pre_in, pre_own, parts,
    back_out, home, whole, z_out, z_in, z_all,
    in_sem, out_sem,
    x_ss, x_rs, p_ss, p_rs, a_ss, a_rs, f_ss, f_rs, o_ss, o_rs, h_ss, h_rs, zr_ss, zr_rs, za_ss, za_rs,
):
    ns, ne, nd = sizes
    s, e, d = lax.axis_index("section"), lax.axis_index("expert"), lax.axis_index("dp")
    cap = x_all.shape[0] // ne
    hid = wg.shape[1]
    per = ne // nd
    y, c = e // 2, e % 2
    ny = ne // 2

    def rows(g):
        return pl.ds(pl.multiple_of(g * cap, cap), cap)

    def expert_peer(k):
        return ((y + k // 2) % ny) * 2 + (c + k) % 2

    def send(src, dst, ss, rs, axis, peer):
        return pltpu.make_async_remote_copy(
            src_ref=src, dst_ref=dst, send_sem=ss, recv_sem=rs,
            device_id={axis: peer}, device_id_type=pl.DeviceIdType.MESH,
        )

    barrier = pltpu.get_barrier_semaphore()
    for axis, me, n in (("section", s, ns), ("expert", e, ne), ("dp", d, nd)):
        for k in range(1, n):
            pl.semaphore_signal(
                barrier, inc=1, device_id={axis: (me + k) % n},
                device_id_type=pl.DeviceIdType.MESH,
            )

    loads = [
        pltpu.make_async_copy(src, dst, in_sem.at[i])
        for i, (src, dst) in enumerate(((wg_hbm, wg), (wu_hbm, wu), (cot_hbm, cot)))
    ]
    for copy in loads:
        copy.start()

    count = tok.shape[0]
    named = lax.broadcasted_iota(jnp.int32, (ne, count), 0)
    member = (named == ids[0:1, :]) | (named == ids[1:2, :])
    before = lax.broadcasted_iota(jnp.int32, (count, count), 0) < lax.broadcasted_iota(
        jnp.int32, (count, count), 1
    )
    rank = dot(
        jnp.where(member, 1.0, 0.0).astype(BF16), jnp.where(before, 1.0, 0.0).astype(BF16), NN
    ).astype(jnp.int32)
    rank = jnp.where(member, rank, -1)
    at = lax.broadcasted_iota(jnp.int32, (cap, count), 0)
    for g in range(ne):
        pick[g * cap : (g + 1) * cap, :] = jnp.where(at == rank[g : g + 1, :], 1.0, 0.0).astype(
            BF16
        )

    def build(g, _):
        x_out[rows(g), :] = dot(pick[rows(g), :], tok[...], NN).astype(BF16)
        return 0

    lax.fori_loop(0, ne, build, 0)
    x_all[rows(e), :] = x_out[rows(e), :]
    pl.semaphore_wait(barrier, ns + ne + nd - 3)

    def x_copy(peer, slot):
        return send(
            x_out.at[rows(peer)], x_all.at[rows(slot)], x_ss.at[peer], x_rs.at[slot],
            "expert", peer,
        )

    near, two_away = (1, 2, 3, 6, 7), (4, 5)
    for k in near:
        x_copy(expert_peer(k), e).start()

    def p_copy(g):
        i = g // nd
        return send(
            pre_out.at[rows(g)], pre_in.at[i, d], p_ss.at[g], p_rs.at[i, d], "dp", g % nd
        )

    for copy in loads[:2]:
        copy.wait()

    def forward(t, _):
        k = jnp.where(t < 4, t, jnp.where(t < 6, t + 2, t - 2))
        g = expert_peer(k)

        @pl.when(t > 0)
        def _():
            x_copy(g, g).wait_recv()

        x = x_all[rows(g), :]
        pg = dot(x, wg[...], NN)
        pu = dot(x, wu[...], NN)

        @pl.when(g % nd == d)
        def _():
            pre_own[g // nd, :, :hid] = pg
            pre_own[g // nd, :, hid:] = pu

        @pl.when(g % nd != d)
        def _():
            pre_out[rows(g), :hid] = pg.astype(BF16)
            pre_out[rows(g), hid:] = pu.astype(BF16)
            p_copy(g).start()

        return 0

    lax.fori_loop(0, 2, forward, 0)
    for k in near:
        x_copy(expert_peer(k), e).wait_send()
    for k in two_away:
        x_copy(expert_peer(k), e).start()
    lax.fori_loop(2, ne, forward, 0)

    right, left = (d + 1) % nd, (d + nd - 1) % nd

    def a_copy(side, g):
        return send(
            parts.at[rows(g)], parts.at[rows(g)], a_ss.at[g // nd, side], a_rs.at[g],
            "dp", left if side else right,
        )

    def f_copy(side, g):
        part = pl.ds(pl.multiple_of(g * cap + side * (cap // 2), cap // 2), cap // 2)
        return send(
            parts.at[part], parts.at[part], f_ss.at[g // nd, side], f_rs.at[g, side],
            "dp", left if side else right,
        )

    def o_copy(peer, g):
        return send(
            acted.at[rows(g)], acted.at[rows(g)], o_ss.at[g // nd, peer], o_rs.at[g], "dp", peer
        )

    loads[2].wait()
    first = y // (ny // per)

    def owned(i):
        total = pre_own[i]
        for k in range(1, nd):
            src = (d + k) % nd
            send(
                pre_out.at[rows(0)], pre_in.at[i, src], p_ss.at[0], p_rs.at[i, src], "dp", src
            ).wait_recv()
            total = total + pre_in[i, src].astype(F32)
        g = i * nd + d
        pre_gate, pre_up = total[:, :hid], total[:, hid:]
        cf = cot[rows(g), :].astype(F32)
        sig = jax.nn.sigmoid(pre_gate)
        silu = pre_gate * sig
        gp = cf * pre_up * sig * (1.0 + pre_gate * (1.0 - sig))
        parts[rows(g), :hid] = gp.astype(BF16)
        parts[rows(g), hid:] = (cf * silu).astype(BF16)
        acted[rows(g), :] = (silu * pre_up).astype(BF16)
        for side in range(2):
            a_copy(side, g).start()

    def h_copy(g):
        return send(back_out.at[rows(g)], home.at[rows(e)], h_ss.at[g], h_rs.at[e], "expert", g)

    def backward(i, k):
        g = i * nd + (d + k) % nd
        if k == 1:
            a_copy(0, g).wait_recv()
            f_copy(1, g).start()
        elif k == nd - 1:
            a_copy(0, g).wait_recv()
            f_copy(0, g).start()
        elif k > 0:
            f_copy(0, g).wait_recv()
            f_copy(1, g).wait_recv()
        back = dot(parts[rows(g), :hid], wg[...], NT) + dot(parts[rows(g), hid:], wu[...], NT)

        @pl.when(g == e)
        def _():
            home[rows(g), :] = back.astype(BF16)

        @pl.when(g != e)
        def _():
            back_out[rows(g), :] = back.astype(BF16)
            h_copy(g).start()

    def wave(t, _):
        i = (first + t) % per
        owned(i)

        @pl.when(t > 0)
        def _():
            backward((first + t + per - 1) % per, 2)

        for k in (0, 1, 3):
            backward(i, k)
        return 0

    lax.fori_loop(0, per, wave, 0)
    backward((first + per - 1) % per, 2)
    for i in range(per):
        for k in range(1, nd):
            o_copy((d + k) % nd, i * nd + d).start()

    tile = 128

    def weights(i, _):
        at = pl.ds(pl.multiple_of(i * tile, tile), tile)
        x = x_all[:, at]
        grad_gate[at, :] = dot(x, parts[:, :hid], TN).astype(BF16)
        grad_up[at, :] = dot(x, parts[:, hid:], TN).astype(BF16)
        return 0

    lax.fori_loop(0, wg.shape[0] // tile, weights, 0)
    stores = [
        pltpu.make_async_copy(src, dst, out_sem.at[i])
        for i, (src, dst) in enumerate(
            ((grad_gate, gate_hbm), (grad_up, up_hbm), (acted, acted_hbm))
        )
    ]
    for copy in stores[:2]:
        copy.start()

    for k in range(1, ne):
        src = expert_peer(k)
        send(
            back_out.at[rows(src)], home.at[rows(src)], h_ss.at[src], h_rs.at[src], "expert", src
        ).wait_recv()
    part = dot(pick[...], home[...], TN).reshape(whole.shape)
    whole[...] = part
    z_out[...] = part.astype(BF16)

    far = [k for j in range(ns // 2, 0, -1) for k in dict.fromkeys((j, ns - j))]

    def zr_copy(peer, slot):
        return send(
            z_out.at[peer], z_in.at[slot], zr_ss.at[peer], zr_rs.at[slot], "section", peer
        )

    def za_copy(peer, slot):
        return send(
            z_all.at[slot], z_all.at[slot], za_ss.at[peer], za_rs.at[slot], "section", peer
        )

    for k in far:
        zr_copy((s + k) % ns, s).start()
    total = whole[s]
    for k in reversed(far):
        src = (s + k) % ns
        zr_copy(src, src).wait_recv()
        total = total + z_in[src].astype(F32)
    z_all[s] = total.astype(BF16)
    for k in far:
        za_copy((s + k) % ns, s).start()
    for i in range(per):
        for k in range(1, nd):
            src = (d + k) % nd
            o_copy(src, i * nd + src).wait_recv()
    stores[2].start()
    for k in reversed(far):
        src = (s + k) % ns
        za_copy(src, src).wait_recv()
    grad_in[...] = z_all[...]

    for k in two_away:
        x_copy(expert_peer(k), e).wait_send()
    for k in range(1, ne):
        h_copy(expert_peer(k)).wait_send()
    for i in range(per):
        for k in range(1, nd):
            p_copy(i * nd + (d + k) % nd).wait_send()
            o_copy((d + k) % nd, i * nd + d).wait_send()
        for side in range(2):
            a_copy(side, i * nd + d).wait_send()
            f_copy(side, i * nd + d).wait_send()
    for k in far:
        zr_copy((s + k) % ns, s).wait_send()
        za_copy((s + k) % ns, s).wait_send()
    for copy in stores:
        copy.wait()


def settle(*refs):
    n = (len(refs) - 2) // 3
    src, dst, held, (in_sem, out_sem) = refs[:n], refs[n : 2 * n], refs[2 * n : 3 * n], refs[3 * n :]
    pieces = in_sem.shape[1]
    reads, writes = [], []
    for i in range(n):
        size = src[i].shape[0] // pieces
        for p in range(pieces):
            at = pl.ds(p * size, size)
            reads.append(
                pltpu.make_async_copy(src[i].at[at], held[i].at[at], in_sem.at[i, p])
            )
            writes.append(
                pltpu.make_async_copy(held[i].at[at], dst[i].at[at], out_sem.at[i, p])
            )
    for copy in reads:
        copy.start()
    for read, write in zip(reads, writes):
        read.wait()
        write.start()
    for copy in writes:
        copy.wait()


def local(tokens, expert_ids, w_gate, w_up, cotangent):
    count, width = tokens.shape
    ns, ne, nd = (lax.axis_size(a) for a in ("section", "expert", "dp"))
    hid = w_gate.shape[2]
    slots = cotangent.shape[1]
    cap = slots // ne
    vmem = pl.BlockSpec(memory_space=pltpu.VMEM)
    dma = pltpu.SemaphoreType.DMA
    share = count // ns
    anywhere = pl.BlockSpec(memory_space=pl.ANY)
    outs = pl.pallas_call(
        lambda *refs: kernel((ns, ne, nd), *refs),
        out_shape=(
            jax.ShapeDtypeStruct((slots, hid), BF16),
            jax.ShapeDtypeStruct((ns, share, width), BF16),
            jax.ShapeDtypeStruct((width, hid), BF16),
            jax.ShapeDtypeStruct((width, hid), BF16),
        ),
        in_specs=[vmem] * 2 + [anywhere] * 3,
        out_specs=(anywhere, vmem, anywhere, anywhere),
        scratch_shapes=[
            pltpu.VMEM((width, hid), BF16),
            pltpu.VMEM((width, hid), BF16),
            pltpu.VMEM((slots, hid), BF16),
            pltpu.VMEM((slots, hid), BF16),
            pltpu.VMEM((width, hid), BF16),
            pltpu.VMEM((width, hid), BF16),
            pltpu.VMEM((slots, count), BF16),
            pltpu.VMEM((slots, width), BF16),
            pltpu.VMEM((slots, width), BF16),
            pltpu.VMEM((slots, 2 * hid), BF16),
            pltpu.VMEM((ne // nd, nd, cap, 2 * hid), BF16),
            pltpu.VMEM((ne // nd, cap, 2 * hid), F32),
            pltpu.VMEM((slots, 2 * hid), BF16),
            pltpu.VMEM((slots, width), BF16),
            pltpu.VMEM((slots, width), BF16),
            pltpu.VMEM((ns, share, width), F32),
            pltpu.VMEM((ns, share, width), BF16),
            pltpu.VMEM((ns, share, width), BF16),
            pltpu.VMEM((ns, share, width), BF16),
            dma((3,)), dma((3,)),
            dma((ne,)), dma((ne,)),
            dma((ne,)), dma((ne // nd, nd)),
            dma((ne // nd, 2)), dma((ne,)),
            dma((ne // nd, 2)), dma((ne, 2)),
            dma((ne // nd, nd)), dma((ne,)),
            dma((ne,)), dma((ne,)),
            dma((ns,)), dma((ns,)),
            dma((ns,)), dma((ns,)),
        ],
        compiler_params=pltpu.CompilerParams(collective_id=0, has_side_effects=True),
    )(tokens, expert_ids.T, w_gate[0], w_up[0], cotangent[0])
    n = len(outs)
    acted, grad_in, grad_gate, grad_up = pl.pallas_call(
        settle,
        out_shape=tuple(jax.ShapeDtypeStruct(o.shape, o.dtype) for o in outs),
        in_specs=[anywhere] * n,
        out_specs=(anywhere,) * n,
        scratch_shapes=[pltpu.VMEM(o.shape, o.dtype) for o in outs] + [dma((n, 4)), dma((n, 4))],
    )(*outs)
    return acted[None], grad_in.reshape(count, width), grad_gate[None], grad_up[None]


def solution(mesh):
    placed = (
        P("expert", "dp"),
        P("expert", None),
        P("expert", "dp", "section"),
        P("expert", "dp", "section"),
        P("expert", None, "section"),
    )
    return jax.shard_map(
        local,
        mesh=mesh,
        in_specs=placed,
        out_specs=(
            P("expert", None, "section"),
            P("expert", "dp"),
            P("expert", "dp", "section"),
            P("expert", "dp", "section"),
        ),
        check_vma=False,
    )
```

```python
import jax
import jax.numpy as jnp
from jax import lax
from jax.experimental import pallas as pl
from jax.experimental.pallas import tpu as pltpu
from jax.sharding import PartitionSpec as P

F32 = jnp.float32
BF16 = jnp.bfloat16
NN = (((1,), (0,)), ((), ()))
NT = (((1,), (1,)), ((), ()))
TN = (((0,), (0,)), ((), ()))


def dot(a, b, dims):
    return lax.dot_general(a, b, dims, preferred_element_type=F32)


def kernel(
    sizes,
    tok, ids, wg_hbm, wu_hbm, cot_hbm,
    acted_hbm, grad_in, gate_hbm, up_hbm,
    wg, wu, cot, acted, grad_gate, grad_up,
    pick, x_out, x_all, pre_out, pre_in, pre_own, parts,
    back_out, home, whole, z_out, z_in, z_all,
    in_sem, out_sem, known,
    x_ss, x_rs, p_ss, p_rs, a_ss, a_rs, f_ss, f_rs, o_ss, o_rs, h_ss, h_rs, zr_ss, zr_rs, za_ss, za_rs,
):
    ns, ne, nd = sizes
    s, e, d = lax.axis_index("section"), lax.axis_index("expert"), lax.axis_index("dp")
    cap = x_all.shape[0] // ne
    hid = wg.shape[1]
    per = ne // nd
    y, c = e // 2, e % 2
    ny = ne // 2

    def rows(g):
        return pl.ds(pl.multiple_of(g * cap, cap), cap)

    def expert_peer(k):
        return ((y + k // 2) % ny) * 2 + (c + k) % 2

    def send(src, dst, ss, rs, axis, peer):
        return pltpu.make_async_remote_copy(
            src_ref=src, dst_ref=dst, send_sem=ss, recv_sem=rs,
            device_id={axis: peer}, device_id_type=pl.DeviceIdType.MESH,
        )

    barrier = pltpu.get_barrier_semaphore()
    rounds = ns // 2 - 1
    greeted = (("section", s, ns, (1, ns - 1)), ("expert", e, ne, range(1, ne)), ("dp", d, nd, range(1, nd)))
    for axis, me, n, offsets in greeted:
        for k in offsets:
            pl.semaphore_signal(
                barrier, inc=1, device_id={axis: (me + k) % n},
                device_id_type=pl.DeviceIdType.MESH,
            )

    loads = [
        pltpu.make_async_copy(src, dst, in_sem.at[i])
        for i, (src, dst) in enumerate(((wg_hbm, wg), (wu_hbm, wu), (cot_hbm, cot)))
    ]
    for copy in loads:
        copy.start()

    count = tok.shape[0]
    named = lax.broadcasted_iota(jnp.int32, (ne, count), 0)
    member = (named == ids[0:1, :]) | (named == ids[1:2, :])
    before = lax.broadcasted_iota(jnp.int32, (count, count), 0) < lax.broadcasted_iota(
        jnp.int32, (count, count), 1
    )
    rank = dot(
        jnp.where(member, 1.0, 0.0).astype(BF16), jnp.where(before, 1.0, 0.0).astype(BF16), NN
    ).astype(jnp.int32)
    rank = jnp.where(member, rank, -1)
    at = lax.broadcasted_iota(jnp.int32, (cap, count), 0)
    for g in range(ne):
        pick[g * cap : (g + 1) * cap, :] = jnp.where(at == rank[g : g + 1, :], 1.0, 0.0).astype(
            BF16
        )

    def build(g):
        x_out[rows(g), :] = dot(pick[rows(g), :], tok[...], NN).astype(BF16)

    def x_copy(peer, slot):
        return send(
            x_out.at[rows(peer)], x_all.at[rows(slot)], x_ss.at[peer], x_rs.at[slot],
            "expert", peer,
        )

    near, two_away = (2, 3, 6, 7, 1), (4, 5)
    build(expert_peer(near[0]))
    pl.semaphore_wait(barrier, sum(len(g[3]) for g in greeted))
    for n, k in enumerate(near):
        if n:
            build(expert_peer(k))
        x_copy(expert_peer(k), e).start()
    x_all[rows(e), :] = dot(pick[rows(e), :], tok[...], NN).astype(BF16)
    for k in two_away:
        build(expert_peer(k))

    def spread(t):
        @pl.when((t > 0) & (t <= rounds))
        def _():
            pl.semaphore_wait(known.at[t - 1], 2)

        @pl.when(t < rounds)
        def _():
            for k in (1, ns - 1):
                pl.semaphore_signal(
                    known.at[t], inc=1, device_id={"section": (s + k) % ns},
                    device_id_type=pl.DeviceIdType.MESH,
                )

    def p_copy(g):
        i = g // nd
        return send(
            pre_out.at[rows(g)], pre_in.at[i, d], p_ss.at[g], p_rs.at[i, d], "dp", g % nd
        )

    for copy in loads[:2]:
        copy.wait()

    def forward(t, _):
        spread(t)
        k = jnp.where(t < 4, t, jnp.where(t < 6, t + 2, t - 2))
        g = expert_peer(k)

        @pl.when(t > 0)
        def _():
            x_copy(g, g).wait_recv()

        x = x_all[rows(g), :]
        pg = dot(x, wg[...], NN)
        pu = dot(x, wu[...], NN)

        @pl.when(g % nd == d)
        def _():
            pre_own[g // nd, :, :hid] = pg
            pre_own[g // nd, :, hid:] = pu

        @pl.when(g % nd != d)
        def _():
            pre_out[rows(g), :hid] = pg.astype(BF16)
            pre_out[rows(g), hid:] = pu.astype(BF16)
            p_copy(g).start()

        return 0

    lax.fori_loop(0, 2, forward, 0)
    for k in near:
        x_copy(expert_peer(k), e).wait_send()
    for k in two_away:
        x_copy(expert_peer(k), e).start()
    lax.fori_loop(2, ne, forward, 0)

    right, left = (d + 1) % nd, (d + nd - 1) % nd

    def a_copy(side, g):
        return send(
            parts.at[rows(g)], parts.at[rows(g)], a_ss.at[g // nd, side], a_rs.at[g],
            "dp", left if side else right,
        )

    def f_copy(side, g):
        part = pl.ds(pl.multiple_of(g * cap + side * (cap // 2), cap // 2), cap // 2)
        return send(
            parts.at[part], parts.at[part], f_ss.at[g // nd, side], f_rs.at[g, side],
            "dp", left if side else right,
        )

    def o_copy(peer, g):
        return send(
            acted.at[rows(g)], acted.at[rows(g)], o_ss.at[g // nd, peer], o_rs.at[g], "dp", peer
        )

    loads[2].wait()
    first = y // (ny // per)

    def owned(i):
        total = pre_own[i]
        for k in range(1, nd):
            src = (d + k) % nd
            send(
                pre_out.at[rows(0)], pre_in.at[i, src], p_ss.at[0], p_rs.at[i, src], "dp", src
            ).wait_recv()
            total = total + pre_in[i, src].astype(F32)
        g = i * nd + d
        pre_gate, pre_up = total[:, :hid], total[:, hid:]
        cf = cot[rows(g), :].astype(F32)
        sig = jax.nn.sigmoid(pre_gate)
        silu = pre_gate * sig
        gp = cf * pre_up * sig * (1.0 + pre_gate * (1.0 - sig))
        parts[rows(g), :hid] = gp.astype(BF16)
        parts[rows(g), hid:] = (cf * silu).astype(BF16)
        acted[rows(g), :] = (silu * pre_up).astype(BF16)
        for side in range(2):
            a_copy(side, g).start()

    def h_copy(g):
        return send(back_out.at[rows(g)], home.at[rows(e)], h_ss.at[g], h_rs.at[e], "expert", g)

    def backward(i, k):
        g = i * nd + (d + k) % nd
        if k == 1:
            a_copy(0, g).wait_recv()
            f_copy(1, g).start()
        elif k == nd - 1:
            a_copy(0, g).wait_recv()
            f_copy(0, g).start()
        elif k > 0:
            f_copy(0, g).wait_recv()
            f_copy(1, g).wait_recv()
        back = dot(parts[rows(g), :hid], wg[...], NT) + dot(parts[rows(g), hid:], wu[...], NT)

        @pl.when(g == e)
        def _():
            home[rows(g), :] = back.astype(BF16)

        @pl.when(g != e)
        def _():
            back_out[rows(g), :] = back.astype(BF16)
            h_copy(g).start()

    def wave(t, _):
        i = (first + t) % per
        owned(i)

        @pl.when(t > 0)
        def _():
            backward((first + t + per - 1) % per, 2)

        for k in (0, 1, 3):
            backward(i, k)
        return 0

    lax.fori_loop(0, per, wave, 0)
    backward((first + per - 1) % per, 2)
    for i in range(per):
        for k in range(1, nd):
            o_copy((d + k) % nd, i * nd + d).start()

    tile = 128

    def weights(i, _):
        at = pl.ds(pl.multiple_of(i * tile, tile), tile)
        x = x_all[:, at]
        grad_gate[at, :] = dot(x, parts[:, :hid], TN).astype(BF16)
        grad_up[at, :] = dot(x, parts[:, hid:], TN).astype(BF16)
        return 0

    lax.fori_loop(0, wg.shape[0] // tile, weights, 0)
    stores = [
        pltpu.make_async_copy(src, dst, out_sem.at[i])
        for i, (src, dst) in enumerate(
            ((grad_gate, gate_hbm), (grad_up, up_hbm), (acted, acted_hbm))
        )
    ]
    for copy in stores[:2]:
        copy.start()

    for k in range(1, ne):
        src = expert_peer(k)
        send(
            back_out.at[rows(src)], home.at[rows(src)], h_ss.at[src], h_rs.at[src], "expert", src
        ).wait_recv()
    part = dot(pick[...], home[...], TN).reshape(whole.shape)
    whole[...] = part
    z_out[...] = part.astype(BF16)

    far = [k for j in range(ns // 2, 0, -1) for k in dict.fromkeys((j, ns - j))]

    def zr_copy(peer, slot):
        return send(
            z_out.at[peer], z_in.at[slot], zr_ss.at[peer], zr_rs.at[slot], "section", peer
        )

    def za_copy(peer, slot):
        return send(
            z_all.at[slot], z_all.at[slot], za_ss.at[peer], za_rs.at[slot], "section", peer
        )

    for k in far:
        zr_copy((s + k) % ns, s).start()
    total = whole[s]
    for k in reversed(far):
        src = (s + k) % ns
        zr_copy(src, src).wait_recv()
        total = total + z_in[src].astype(F32)
    z_all[s] = total.astype(BF16)
    for k in far:
        za_copy((s + k) % ns, s).start()
    for i in range(per):
        for k in range(1, nd):
            src = (d + k) % nd
            o_copy(src, i * nd + src).wait_recv()
    stores[2].start()
    for k in reversed(far):
        src = (s + k) % ns
        za_copy(src, src).wait_recv()
    grad_in[...] = z_all[...]

    for k in two_away:
        x_copy(expert_peer(k), e).wait_send()
    for k in range(1, ne):
        h_copy(expert_peer(k)).wait_send()
    for i in range(per):
        for k in range(1, nd):
            p_copy(i * nd + (d + k) % nd).wait_send()
            o_copy((d + k) % nd, i * nd + d).wait_send()
        for side in range(2):
            a_copy(side, i * nd + d).wait_send()
            f_copy(side, i * nd + d).wait_send()
    for k in far:
        zr_copy((s + k) % ns, s).wait_send()
        za_copy((s + k) % ns, s).wait_send()
    for copy in stores:
        copy.wait()


def settle(*refs):
    n = (len(refs) - 2) // 3
    src, dst, held, (in_sem, out_sem) = refs[:n], refs[n : 2 * n], refs[2 * n : 3 * n], refs[3 * n :]
    pieces = in_sem.shape[1]
    reads, writes = [], []
    for i in range(n):
        size = src[i].shape[0] // pieces
        for p in range(pieces):
            at = pl.ds(p * size, size)
            reads.append(
                pltpu.make_async_copy(src[i].at[at], held[i].at[at], in_sem.at[i, p])
            )
            writes.append(
                pltpu.make_async_copy(held[i].at[at], dst[i].at[at], out_sem.at[i, p])
            )
    for copy in reads:
        copy.start()
    for read, write in zip(reads, writes):
        read.wait()
        write.start()
    for copy in writes:
        copy.wait()


def local(tokens, expert_ids, w_gate, w_up, cotangent):
    count, width = tokens.shape
    ns, ne, nd = (lax.axis_size(a) for a in ("section", "expert", "dp"))
    hid = w_gate.shape[2]
    slots = cotangent.shape[1]
    cap = slots // ne
    vmem = pl.BlockSpec(memory_space=pltpu.VMEM)
    dma = pltpu.SemaphoreType.DMA
    share = count // ns
    anywhere = pl.BlockSpec(memory_space=pl.ANY)
    outs = pl.pallas_call(
        lambda *refs: kernel((ns, ne, nd), *refs),
        out_shape=(
            jax.ShapeDtypeStruct((slots, hid), BF16),
            jax.ShapeDtypeStruct((ns, share, width), BF16),
            jax.ShapeDtypeStruct((width, hid), BF16),
            jax.ShapeDtypeStruct((width, hid), BF16),
        ),
        in_specs=[vmem] * 2 + [anywhere] * 3,
        out_specs=(anywhere, vmem, anywhere, anywhere),
        scratch_shapes=[
            pltpu.VMEM((width, hid), BF16),
            pltpu.VMEM((width, hid), BF16),
            pltpu.VMEM((slots, hid), BF16),
            pltpu.VMEM((slots, hid), BF16),
            pltpu.VMEM((width, hid), BF16),
            pltpu.VMEM((width, hid), BF16),
            pltpu.VMEM((slots, count), BF16),
            pltpu.VMEM((slots, width), BF16),
            pltpu.VMEM((slots, width), BF16),
            pltpu.VMEM((slots, 2 * hid), BF16),
            pltpu.VMEM((ne // nd, nd, cap, 2 * hid), BF16),
            pltpu.VMEM((ne // nd, cap, 2 * hid), F32),
            pltpu.VMEM((slots, 2 * hid), BF16),
            pltpu.VMEM((slots, width), BF16),
            pltpu.VMEM((slots, width), BF16),
            pltpu.VMEM((ns, share, width), F32),
            pltpu.VMEM((ns, share, width), BF16),
            pltpu.VMEM((ns, share, width), BF16),
            pltpu.VMEM((ns, share, width), BF16),
            dma((3,)), dma((3,)), pltpu.SemaphoreType.REGULAR((ns // 2 - 1,)),
            dma((ne,)), dma((ne,)),
            dma((ne,)), dma((ne // nd, nd)),
            dma((ne // nd, 2)), dma((ne,)),
            dma((ne // nd, 2)), dma((ne, 2)),
            dma((ne // nd, nd)), dma((ne,)),
            dma((ne,)), dma((ne,)),
            dma((ns,)), dma((ns,)),
            dma((ns,)), dma((ns,)),
        ],
        compiler_params=pltpu.CompilerParams(collective_id=0, has_side_effects=True),
    )(tokens, expert_ids.T, w_gate[0], w_up[0], cotangent[0])
    n = len(outs)
    acted, grad_in, grad_gate, grad_up = pl.pallas_call(
        settle,
        out_shape=tuple(jax.ShapeDtypeStruct(o.shape, o.dtype) for o in outs),
        in_specs=[anywhere] * n,
        out_specs=(anywhere,) * n,
        scratch_shapes=[pltpu.VMEM(o.shape, o.dtype) for o in outs] + [dma((n, 4)), dma((n, 4))],
    )(*outs)
    return acted[None], grad_in.reshape(count, width), grad_gate[None], grad_up[None]


def solution(mesh):
    placed = (
        P("expert", "dp"),
        P("expert", None),
        P("expert", "dp", "section"),
        P("expert", "dp", "section"),
        P("expert", None, "section"),
    )
    return jax.shard_map(
        local,
        mesh=mesh,
        in_specs=placed,
        out_specs=(
            P("expert", None, "section"),
            P("expert", "dp"),
            P("expert", "dp", "section"),
            P("expert", "dp", "section"),
        ),
        check_vma=False,
    )
```

```python
import jax
import jax.numpy as jnp
from jax import lax
from jax.experimental import pallas as pl
from jax.experimental.pallas import tpu as pltpu
from jax.sharding import PartitionSpec as P

F32 = jnp.float32
BF16 = jnp.bfloat16
NN = (((1,), (0,)), ((), ()))
NT = (((1,), (1,)), ((), ()))
TN = (((0,), (0,)), ((), ()))


def dot(a, b, dims):
    return lax.dot_general(a, b, dims, preferred_element_type=F32)


def kernel(
    sizes,
    tok, ids, wg_hbm, wu_hbm, cot_hbm,
    acted_hbm, grad_in, gate_hbm, up_hbm,
    wg, wu, cot, acted, grad_gate, grad_up,
    pick, x_out, x_all, pre_out, pre_in, pre_own, parts,
    back_out, home, whole, z_out, z_in, z_all,
    in_sem, out_sem, known,
    x_ss, x_rs, p_ss, p_rs, a_ss, a_rs, f_ss, f_rs, o_ss, o_rs, h_ss, h_rs, zr_ss, zr_rs, za_ss, za_rs,
):
    ns, ne, nd = sizes
    s, e, d = lax.axis_index("section"), lax.axis_index("expert"), lax.axis_index("dp")
    cap = x_all.shape[0] // ne
    hid = wg.shape[1]
    per = ne // nd
    y, c = e // 2, e % 2
    ny = ne // 2

    def rows(g):
        return pl.ds(pl.multiple_of(g * cap, cap), cap)

    def expert_peer(k):
        return ((y + k // 2) % ny) * 2 + (c + k) % 2

    def send(src, dst, ss, rs, axis, peer):
        return pltpu.make_async_remote_copy(
            src_ref=src, dst_ref=dst, send_sem=ss, recv_sem=rs,
            device_id={axis: peer}, device_id_type=pl.DeviceIdType.MESH,
        )

    barrier = pltpu.get_barrier_semaphore()
    rounds = ns // 2 - 1
    greeted = (("section", s, ns, (1, ns - 1)), ("expert", e, ne, range(1, ne)), ("dp", d, nd, range(1, nd)))
    for axis, me, n, offsets in greeted:
        for k in offsets:
            pl.semaphore_signal(
                barrier, inc=1, device_id={axis: (me + k) % n},
                device_id_type=pl.DeviceIdType.MESH,
            )

    loads = [
        pltpu.make_async_copy(src, dst, in_sem.at[i])
        for i, (src, dst) in enumerate(((wg_hbm, wg), (wu_hbm, wu), (cot_hbm, cot)))
    ]
    for copy in loads:
        copy.start()

    count = tok.shape[0]
    named = lax.broadcasted_iota(jnp.int32, (ne, count), 0)
    member = (named == ids[0:1, :]) | (named == ids[1:2, :])
    before = lax.broadcasted_iota(jnp.int32, (count, count), 0) < lax.broadcasted_iota(
        jnp.int32, (count, count), 1
    )
    rank = dot(
        jnp.where(member, 1.0, 0.0).astype(BF16), jnp.where(before, 1.0, 0.0).astype(BF16), NN
    ).astype(jnp.int32)
    rank = jnp.where(member, rank, -1)
    at = lax.broadcasted_iota(jnp.int32, (cap, count), 0)
    for g in range(ne):
        pick[g * cap : (g + 1) * cap, :] = jnp.where(at == rank[g : g + 1, :], 1.0, 0.0).astype(
            BF16
        )

    def build(g):
        x_out[rows(g), :] = dot(pick[rows(g), :], tok[...], NN).astype(BF16)

    def x_copy(peer, slot):
        return send(
            x_out.at[rows(peer)], x_all.at[rows(slot)], x_ss.at[peer], x_rs.at[slot],
            "expert", peer,
        )

    near, two_away = (2, 3, 6, 7, 1), (4, 5)
    build(expert_peer(near[0]))
    pl.semaphore_wait(barrier, sum(len(g[3]) for g in greeted))
    for n, k in enumerate(near):
        if n:
            build(expert_peer(k))
        x_copy(expert_peer(k), e).start()
    x_all[rows(e), :] = dot(pick[rows(e), :], tok[...], NN).astype(BF16)
    for k in two_away:
        build(expert_peer(k))

    def spread(t):
        @pl.when((t > 0) & (t <= rounds))
        def _():
            pl.semaphore_wait(known.at[t - 1], 2)

        @pl.when(t < rounds)
        def _():
            for k in (1, ns - 1):
                pl.semaphore_signal(
                    known.at[t], inc=1, device_id={"section": (s + k) % ns},
                    device_id_type=pl.DeviceIdType.MESH,
                )

    def p_copy(g):
        i = g // nd
        return send(
            pre_out.at[rows(g)], pre_in.at[i, d], p_ss.at[g], p_rs.at[i, d], "dp", g % nd
        )

    for copy in loads[:2]:
        copy.wait()

    def forward(t, _):
        spread(t)
        k = jnp.where(
            t < 2, t, jnp.where(t < 4, 4 * (y % 2) + t, jnp.where(t < 6, 2 - 4 * (y % 2) + t, t - 2))
        )
        g = expert_peer(k)

        @pl.when(t > 0)
        def _():
            x_copy(g, g).wait_recv()

        x = x_all[rows(g), :]
        pg = dot(x, wg[...], NN)
        pu = dot(x, wu[...], NN)

        @pl.when(g % nd == d)
        def _():
            pre_own[g // nd, :, :hid] = pg
            pre_own[g // nd, :, hid:] = pu

        @pl.when(g % nd != d)
        def _():
            pre_out[rows(g), :hid] = pg.astype(BF16)
            pre_out[rows(g), hid:] = pu.astype(BF16)

        @pl.when(t == ne // 2)
        def _():
            for k in range(1, nd):
                p_copy(first * nd + (d + k) % nd).wait_send()

        @pl.when(g % nd != d)
        def _():
            p_copy(g).start()

        return 0

    first = y // (ny // per)

    lax.fori_loop(0, 2, forward, 0)
    for k in near:
        x_copy(expert_peer(k), e).wait_send()
    for k in two_away:
        x_copy(expert_peer(k), e).start()
    lax.fori_loop(2, ne, forward, 0)

    right, left = (d + 1) % nd, (d + nd - 1) % nd

    def a_copy(side, g):
        return send(
            parts.at[rows(g)], parts.at[rows(g)], a_ss.at[g // nd, side], a_rs.at[g],
            "dp", left if side else right,
        )

    def f_copy(side, g):
        part = pl.ds(pl.multiple_of(g * cap + side * (cap // 2), cap // 2), cap // 2)
        return send(
            parts.at[part], parts.at[part], f_ss.at[g // nd, side], f_rs.at[g, side],
            "dp", left if side else right,
        )

    def o_copy(peer, g):
        return send(
            acted.at[rows(g)], acted.at[rows(g)], o_ss.at[g // nd, peer], o_rs.at[g], "dp", peer
        )

    loads[2].wait()

    def owned(i):
        total = pre_own[i]
        for k in range(1, nd):
            src = (d + k) % nd
            send(
                pre_out.at[rows(0)], pre_in.at[i, src], p_ss.at[0], p_rs.at[i, src], "dp", src
            ).wait_recv()
            total = total + pre_in[i, src].astype(F32)
        g = i * nd + d
        pre_gate, pre_up = total[:, :hid], total[:, hid:]
        cf = cot[rows(g), :].astype(F32)
        sig = jax.nn.sigmoid(pre_gate)
        silu = pre_gate * sig
        gp = cf * pre_up * sig * (1.0 + pre_gate * (1.0 - sig))
        parts[rows(g), :hid] = gp.astype(BF16)
        parts[rows(g), hid:] = (cf * silu).astype(BF16)
        acted[rows(g), :] = (silu * pre_up).astype(BF16)
        for side in range(2):
            a_copy(side, g).start()

    def h_copy(g):
        return send(back_out.at[rows(g)], home.at[rows(e)], h_ss.at[g], h_rs.at[e], "expert", g)

    def backward(i, k):
        g = i * nd + (d + k) % nd
        if k == 1:
            a_copy(0, g).wait_recv()
            f_copy(1, g).start()
        elif k == nd - 1:
            a_copy(0, g).wait_recv()
            f_copy(0, g).start()
        elif k > 0:
            f_copy(0, g).wait_recv()
            f_copy(1, g).wait_recv()
        back = dot(parts[rows(g), :hid], wg[...], NT) + dot(parts[rows(g), hid:], wu[...], NT)

        @pl.when(g == e)
        def _():
            home[rows(g), :] = back.astype(BF16)

        @pl.when(g != e)
        def _():
            back_out[rows(g), :] = back.astype(BF16)
            h_copy(g).start()

    def wave(t, _):
        i = (first + t) % per
        owned(i)

        @pl.when(t > 0)
        def _():
            backward((first + t + per - 1) % per, 2)

        for k in (0, 1, 3):
            backward(i, k)
        return 0

    lax.fori_loop(0, per, wave, 0)
    backward((first + per - 1) % per, 2)
    for i in range(per):
        for k in range(1, nd):
            o_copy((d + k) % nd, i * nd + d).start()

    for k in range(1, ne):
        src = expert_peer(k)
        send(
            back_out.at[rows(src)], home.at[rows(src)], h_ss.at[src], h_rs.at[src], "expert", src
        ).wait_recv()
    part = dot(pick[...], home[...], TN).reshape(whole.shape)
    whole[...] = part
    z_out[...] = part.astype(BF16)

    far = [k for j in range(ns // 2, 0, -1) for k in dict.fromkeys((j, ns - j))]

    def zr_copy(peer, slot):
        return send(
            z_out.at[peer], z_in.at[slot], zr_ss.at[peer], zr_rs.at[slot], "section", peer
        )

    def za_copy(peer, slot):
        return send(
            z_all.at[slot], z_all.at[slot], za_ss.at[peer], za_rs.at[slot], "section", peer
        )

    for k in far:
        zr_copy((s + k) % ns, s).start()

    tile = 128

    def weights(i, _):
        at = pl.ds(pl.multiple_of(i * tile, tile), tile)
        x = x_all[:, at]
        grad_gate[at, :] = dot(x, parts[:, :hid], TN).astype(BF16)
        grad_up[at, :] = dot(x, parts[:, hid:], TN).astype(BF16)
        return 0

    lax.fori_loop(0, wg.shape[0] // tile, weights, 0)
    stores = [
        pltpu.make_async_copy(src, dst, out_sem.at[i])
        for i, (src, dst) in enumerate(
            ((grad_gate, gate_hbm), (grad_up, up_hbm), (acted, acted_hbm))
        )
    ]
    for copy in stores[:2]:
        copy.start()

    total = whole[s]
    for k in reversed(far):
        src = (s + k) % ns
        zr_copy(src, src).wait_recv()
        total = total + z_in[src].astype(F32)
    z_all[s] = total.astype(BF16)
    for k in far:
        za_copy((s + k) % ns, s).start()
    for i in range(per):
        for k in range(1, nd):
            src = (d + k) % nd
            o_copy(src, i * nd + src).wait_recv()
    stores[2].start()
    for k in reversed(far):
        src = (s + k) % ns
        za_copy(src, src).wait_recv()
    grad_in[...] = z_all[...]

    for k in two_away:
        x_copy(expert_peer(k), e).wait_send()
    for k in range(1, ne):
        h_copy(expert_peer(k)).wait_send()
    for k in range(1, nd):
        p_copy((first + 1) % per * nd + (d + k) % nd).wait_send()
    for i in range(per):
        for k in range(1, nd):
            o_copy((d + k) % nd, i * nd + d).wait_send()
        for side in range(2):
            a_copy(side, i * nd + d).wait_send()
            f_copy(side, i * nd + d).wait_send()
    for k in far:
        zr_copy((s + k) % ns, s).wait_send()
        za_copy((s + k) % ns, s).wait_send()
    for copy in stores:
        copy.wait()


def settle(*refs):
    n = (len(refs) - 2) // 3
    src, dst, held, (in_sem, out_sem) = refs[:n], refs[n : 2 * n], refs[2 * n : 3 * n], refs[3 * n :]
    pieces = in_sem.shape[1]
    reads, writes = [], []
    for i in range(n):
        size = src[i].shape[0] // pieces
        for p in range(pieces):
            at = pl.ds(p * size, size)
            reads.append(
                pltpu.make_async_copy(src[i].at[at], held[i].at[at], in_sem.at[i, p])
            )
            writes.append(
                pltpu.make_async_copy(held[i].at[at], dst[i].at[at], out_sem.at[i, p])
            )
    for copy in reads:
        copy.start()
    for read, write in zip(reads, writes):
        read.wait()
        write.start()
    for copy in writes:
        copy.wait()


def local(tokens, expert_ids, w_gate, w_up, cotangent):
    count, width = tokens.shape
    ns, ne, nd = (lax.axis_size(a) for a in ("section", "expert", "dp"))
    hid = w_gate.shape[2]
    slots = cotangent.shape[1]
    cap = slots // ne
    vmem = pl.BlockSpec(memory_space=pltpu.VMEM)
    dma = pltpu.SemaphoreType.DMA
    share = count // ns
    anywhere = pl.BlockSpec(memory_space=pl.ANY)
    outs = pl.pallas_call(
        lambda *refs: kernel((ns, ne, nd), *refs),
        out_shape=(
            jax.ShapeDtypeStruct((slots, hid), BF16),
            jax.ShapeDtypeStruct((ns, share, width), BF16),
            jax.ShapeDtypeStruct((width, hid), BF16),
            jax.ShapeDtypeStruct((width, hid), BF16),
        ),
        in_specs=[vmem] * 2 + [anywhere] * 3,
        out_specs=(anywhere, vmem, anywhere, anywhere),
        scratch_shapes=[
            pltpu.VMEM((width, hid), BF16),
            pltpu.VMEM((width, hid), BF16),
            pltpu.VMEM((slots, hid), BF16),
            pltpu.VMEM((slots, hid), BF16),
            pltpu.VMEM((width, hid), BF16),
            pltpu.VMEM((width, hid), BF16),
            pltpu.VMEM((slots, count), BF16),
            pltpu.VMEM((slots, width), BF16),
            pltpu.VMEM((slots, width), BF16),
            pltpu.VMEM((slots, 2 * hid), BF16),
            pltpu.VMEM((ne // nd, nd, cap, 2 * hid), BF16),
            pltpu.VMEM((ne // nd, cap, 2 * hid), F32),
            pltpu.VMEM((slots, 2 * hid), BF16),
            pltpu.VMEM((slots, width), BF16),
            pltpu.VMEM((slots, width), BF16),
            pltpu.VMEM((ns, share, width), F32),
            pltpu.VMEM((ns, share, width), BF16),
            pltpu.VMEM((ns, share, width), BF16),
            pltpu.VMEM((ns, share, width), BF16),
            dma((3,)), dma((3,)), pltpu.SemaphoreType.REGULAR((ns // 2 - 1,)),
            dma((ne,)), dma((ne,)),
            dma((ne,)), dma((ne // nd, nd)),
            dma((ne // nd, 2)), dma((ne,)),
            dma((ne // nd, 2)), dma((ne, 2)),
            dma((ne // nd, nd)), dma((ne,)),
            dma((ne,)), dma((ne,)),
            dma((ns,)), dma((ns,)),
            dma((ns,)), dma((ns,)),
        ],
        compiler_params=pltpu.CompilerParams(collective_id=0, has_side_effects=True),
    )(tokens, expert_ids.T, w_gate[0], w_up[0], cotangent[0])
    n = len(outs)
    acted, grad_in, grad_gate, grad_up = pl.pallas_call(
        settle,
        out_shape=tuple(jax.ShapeDtypeStruct(o.shape, o.dtype) for o in outs),
        in_specs=[anywhere] * n,
        out_specs=(anywhere,) * n,
        scratch_shapes=[pltpu.VMEM(o.shape, o.dtype) for o in outs] + [dma((n, 4)), dma((n, 4))],
    )(*outs)
    return acted[None], grad_in.reshape(count, width), grad_gate[None], grad_up[None]


def solution(mesh):
    placed = (
        P("expert", "dp"),
        P("expert", None),
        P("expert", "dp", "section"),
        P("expert", "dp", "section"),
        P("expert", None, "section"),
    )
    return jax.shard_map(
        local,
        mesh=mesh,
        in_specs=placed,
        out_specs=(
            P("expert", None, "section"),
            P("expert", "dp"),
            P("expert", "dp", "section"),
            P("expert", "dp", "section"),
        ),
        check_vma=False,
    )
```

```python
import jax
import jax.numpy as jnp
from jax import lax
from jax.experimental import pallas as pl
from jax.experimental.pallas import tpu as pltpu
from jax.sharding import PartitionSpec as P

F32 = jnp.float32
BF16 = jnp.bfloat16
NN = (((1,), (0,)), ((), ()))
NT = (((1,), (1,)), ((), ()))
TN = (((0,), (0,)), ((), ()))


def dot(a, b, dims):
    return lax.dot_general(a, b, dims, preferred_element_type=F32)


def kernel(
    sizes,
    tok, ids, wg_hbm, wu_hbm, cot_hbm,
    acted_hbm, grad_in, gate_hbm, up_hbm,
    wg, wu, cot, acted, grad_gate, grad_up,
    pick, x_out, x_all, pre_out, pre_in, pre_own, parts,
    back_out, home, whole, z_out, z_in, z_all,
    in_sem, out_sem, known,
    x_ss, x_rs, p_ss, p_rs, a_ss, a_rs, f_ss, f_rs, o_ss, o_rs, h_ss, h_rs, zr_ss, zr_rs, za_ss, za_rs,
):
    ns, ne, nd = sizes
    s, e, d = lax.axis_index("section"), lax.axis_index("expert"), lax.axis_index("dp")
    cap = x_all.shape[0] // ne
    hid = wg.shape[1]
    per = ne // nd
    y, c = e // 2, e % 2
    ny = ne // 2

    def rows(g):
        return pl.ds(pl.multiple_of(g * cap, cap), cap)

    def expert_peer(k):
        return ((y + k // 2) % ny) * 2 + (c + k) % 2

    def send(src, dst, ss, rs, axis, peer):
        return pltpu.make_async_remote_copy(
            src_ref=src, dst_ref=dst, send_sem=ss, recv_sem=rs,
            device_id={axis: peer}, device_id_type=pl.DeviceIdType.MESH,
        )

    barrier = pltpu.get_barrier_semaphore()
    rounds = ns // 2 - 1
    greeted = (("section", s, ns, (1, ns - 1)), ("expert", e, ne, range(1, ne)), ("dp", d, nd, range(1, nd)))
    for axis, me, n, offsets in greeted:
        for k in offsets:
            pl.semaphore_signal(
                barrier, inc=1, device_id={axis: (me + k) % n},
                device_id_type=pl.DeviceIdType.MESH,
            )

    loads = [
        pltpu.make_async_copy(src, dst, in_sem.at[i])
        for i, (src, dst) in enumerate(((wg_hbm, wg), (wu_hbm, wu), (cot_hbm, cot)))
    ]
    for copy in loads:
        copy.start()

    count = tok.shape[0]
    named = lax.broadcasted_iota(jnp.int32, (ne, count), 0)
    member = (named == ids[0:1, :]) | (named == ids[1:2, :])
    before = lax.broadcasted_iota(jnp.int32, (count, count), 0) < lax.broadcasted_iota(
        jnp.int32, (count, count), 1
    )
    rank = dot(
        jnp.where(member, 1.0, 0.0).astype(BF16), jnp.where(before, 1.0, 0.0).astype(BF16), NN
    ).astype(jnp.int32)
    rank = jnp.where(member, rank, -1)
    at = lax.broadcasted_iota(jnp.int32, (cap, count), 0)
    for g in range(ne):
        pick[g * cap : (g + 1) * cap, :] = jnp.where(at == rank[g : g + 1, :], 1.0, 0.0).astype(
            BF16
        )

    def build(g):
        x_out[rows(g), :] = dot(pick[rows(g), :], tok[...], NN).astype(BF16)

    def x_copy(peer, slot):
        return send(
            x_out.at[rows(peer)], x_all.at[rows(slot)], x_ss.at[peer], x_rs.at[slot],
            "expert", peer,
        )

    near, two_away = (2, 3, 6, 7, 1), (4, 5)
    build(expert_peer(near[0]))
    pl.semaphore_wait(barrier, sum(len(g[3]) for g in greeted))
    for n, k in enumerate(near):
        if n:
            build(expert_peer(k))
        x_copy(expert_peer(k), e).start()
    x_all[rows(e), :] = dot(pick[rows(e), :], tok[...], NN).astype(BF16)
    for k in two_away:
        build(expert_peer(k))

    def spread(t):
        @pl.when((t > 0) & (t <= rounds))
        def _():
            pl.semaphore_wait(known.at[t - 1], 2)

        @pl.when(t < rounds)
        def _():
            for k in (1, ns - 1):
                pl.semaphore_signal(
                    known.at[t], inc=1, device_id={"section": (s + k) % ns},
                    device_id_type=pl.DeviceIdType.MESH,
                )

    def p_copy(g):
        i = g // nd
        return send(
            pre_out.at[rows(g)], pre_in.at[i, d], p_ss.at[g], p_rs.at[i, d], "dp", g % nd
        )

    for copy in loads[:2]:
        copy.wait()

    def forward(t, _):
        spread(t)
        k = jnp.where(
            t < 2, t, jnp.where(t < 4, 4 * (y % 2) + t, jnp.where(t < 6, 2 - 4 * (y % 2) + t, t - 2))
        )
        g = expert_peer(k)

        @pl.when(t > 0)
        def _():
            x_copy(g, g).wait_recv()

        x = x_all[rows(g), :]
        pg = dot(x, wg[...], NN)
        pu = dot(x, wu[...], NN)

        @pl.when(g % nd == d)
        def _():
            pre_own[g // nd, :, :hid] = pg
            pre_own[g // nd, :, hid:] = pu

        @pl.when(g % nd != d)
        def _():
            pre_out[rows(g), :hid] = pg.astype(BF16)
            pre_out[rows(g), hid:] = pu.astype(BF16)

        @pl.when(t == ne // 2)
        def _():
            for k in range(1, nd):
                p_copy(first * nd + (d + k) % nd).wait_send()

        @pl.when(g % nd != d)
        def _():
            p_copy(g).start()

        return 0

    first = y // (ny // per)

    lax.fori_loop(0, 2, forward, 0)
    for k in near:
        x_copy(expert_peer(k), e).wait_send()
    for k in two_away:
        x_copy(expert_peer(k), e).start()
    lax.fori_loop(2, ne, forward, 0)

    right, left = (d + 1) % nd, (d + nd - 1) % nd

    def a_copy(side, g):
        return send(
            parts.at[rows(g)], parts.at[rows(g)], a_ss.at[g // nd, side], a_rs.at[g],
            "dp", left if side else right,
        )

    def f_copy(side, g):
        part = pl.ds(pl.multiple_of(g * cap + side * (cap // 2), cap // 2), cap // 2)
        return send(
            parts.at[part], parts.at[part], f_ss.at[g // nd, side], f_rs.at[g, side],
            "dp", left if side else right,
        )

    def o_copy(peer, g):
        return send(
            acted.at[rows(g)], acted.at[rows(g)], o_ss.at[g // nd, peer], o_rs.at[g], "dp", peer
        )

    loads[2].wait()

    def owned(i):
        total = pre_own[i]
        for k in range(1, nd):
            src = (d + k) % nd
            send(
                pre_out.at[rows(0)], pre_in.at[i, src], p_ss.at[0], p_rs.at[i, src], "dp", src
            ).wait_recv()
            total = total + pre_in[i, src].astype(F32)
        g = i * nd + d
        pre_gate, pre_up = total[:, :hid], total[:, hid:]
        cf = cot[rows(g), :].astype(F32)
        sig = jax.nn.sigmoid(pre_gate)
        silu = pre_gate * sig
        gp = cf * pre_up * sig * (1.0 + pre_gate * (1.0 - sig))
        parts[rows(g), :hid] = gp.astype(BF16)
        parts[rows(g), hid:] = (cf * silu).astype(BF16)
        acted[rows(g), :] = (silu * pre_up).astype(BF16)
        for side in range(2):
            a_copy(side, g).start()

    def h_copy(g):
        return send(back_out.at[rows(g)], home.at[rows(e)], h_ss.at[g], h_rs.at[e], "expert", g)

    def backward(i, k):
        g = i * nd + (d + k) % nd
        if k == 1:
            a_copy(0, g).wait_recv()
            f_copy(1, g).start()
        elif k == nd - 1:
            a_copy(0, g).wait_recv()
            f_copy(0, g).start()
        elif k > 0:
            f_copy(0, g).wait_recv()
            f_copy(1, g).wait_recv()
        back = dot(parts[rows(g), :hid], wg[...], NT) + dot(parts[rows(g), hid:], wu[...], NT)

        @pl.when(g == e)
        def _():
            home[rows(g), :] = back.astype(BF16)

        @pl.when(g != e)
        def _():
            back_out[rows(g), :] = back.astype(BF16)
            h_copy(g).start()

    def mine(t, _):
        i = (first + t) % per
        owned(i)
        backward(i, 0)
        return 0

    def beside(t, _):
        i = (first + t) % per
        backward(i, 1)
        backward(i, 3)
        return 0

    def opposite(t, _):
        backward((first + t) % per, 2)
        return 0

    for step in (mine, beside, opposite):
        lax.fori_loop(0, per, step, 0)
    for i in range(per):
        for k in range(1, nd):
            o_copy((d + k) % nd, i * nd + d).start()

    for k in range(1, ne):
        src = expert_peer(k)
        send(
            back_out.at[rows(src)], home.at[rows(src)], h_ss.at[src], h_rs.at[src], "expert", src
        ).wait_recv()
    part = dot(pick[...], home[...], TN).reshape(whole.shape)
    whole[...] = part
    z_out[...] = part.astype(BF16)

    far = [k for j in range(ns // 2, 0, -1) for k in dict.fromkeys((j, ns - j))]

    def zr_copy(peer, slot):
        return send(
            z_out.at[peer], z_in.at[slot], zr_ss.at[peer], zr_rs.at[slot], "section", peer
        )

    def za_copy(peer, slot):
        return send(
            z_all.at[slot], z_all.at[slot], za_ss.at[peer], za_rs.at[slot], "section", peer
        )

    for k in far:
        zr_copy((s + k) % ns, s).start()

    tile = 128

    def weights(i, _):
        at = pl.ds(pl.multiple_of(i * tile, tile), tile)
        x = x_all[:, at]
        grad_gate[at, :] = dot(x, parts[:, :hid], TN).astype(BF16)
        grad_up[at, :] = dot(x, parts[:, hid:], TN).astype(BF16)
        return 0

    lax.fori_loop(0, wg.shape[0] // tile, weights, 0)
    stores = [
        pltpu.make_async_copy(src, dst, out_sem.at[i])
        for i, (src, dst) in enumerate(
            ((grad_gate, gate_hbm), (grad_up, up_hbm), (acted, acted_hbm))
        )
    ]
    for copy in stores[:2]:
        copy.start()

    total = whole[s]
    for k in reversed(far):
        src = (s + k) % ns
        zr_copy(src, src).wait_recv()
        total = total + z_in[src].astype(F32)
    z_all[s] = total.astype(BF16)
    for k in far:
        za_copy((s + k) % ns, s).start()
    for i in range(per):
        for k in range(1, nd):
            src = (d + k) % nd
            o_copy(src, i * nd + src).wait_recv()
    stores[2].start()
    for k in reversed(far):
        src = (s + k) % ns
        za_copy(src, src).wait_recv()
    grad_in[...] = z_all[...]

    for k in two_away:
        x_copy(expert_peer(k), e).wait_send()
    for k in range(1, ne):
        h_copy(expert_peer(k)).wait_send()
    for k in range(1, nd):
        p_copy((first + 1) % per * nd + (d + k) % nd).wait_send()
    for i in range(per):
        for k in range(1, nd):
            o_copy((d + k) % nd, i * nd + d).wait_send()
        for side in range(2):
            a_copy(side, i * nd + d).wait_send()
            f_copy(side, i * nd + d).wait_send()
    for k in far:
        zr_copy((s + k) % ns, s).wait_send()
        za_copy((s + k) % ns, s).wait_send()
    for copy in stores:
        copy.wait()


def settle(*refs):
    n = (len(refs) - 2) // 3
    src, dst, held, (in_sem, out_sem) = refs[:n], refs[n : 2 * n], refs[2 * n : 3 * n], refs[3 * n :]
    pieces = in_sem.shape[1]
    reads, writes = [], []
    for i in range(n):
        size = src[i].shape[0] // pieces
        for p in range(pieces):
            at = pl.ds(p * size, size)
            reads.append(
                pltpu.make_async_copy(src[i].at[at], held[i].at[at], in_sem.at[i, p])
            )
            writes.append(
                pltpu.make_async_copy(held[i].at[at], dst[i].at[at], out_sem.at[i, p])
            )
    for copy in reads:
        copy.start()
    for read, write in zip(reads, writes):
        read.wait()
        write.start()
    for copy in writes:
        copy.wait()


def local(tokens, expert_ids, w_gate, w_up, cotangent):
    count, width = tokens.shape
    ns, ne, nd = (lax.axis_size(a) for a in ("section", "expert", "dp"))
    hid = w_gate.shape[2]
    slots = cotangent.shape[1]
    cap = slots // ne
    vmem = pl.BlockSpec(memory_space=pltpu.VMEM)
    dma = pltpu.SemaphoreType.DMA
    share = count // ns
    anywhere = pl.BlockSpec(memory_space=pl.ANY)
    outs = pl.pallas_call(
        lambda *refs: kernel((ns, ne, nd), *refs),
        out_shape=(
            jax.ShapeDtypeStruct((slots, hid), BF16),
            jax.ShapeDtypeStruct((ns, share, width), BF16),
            jax.ShapeDtypeStruct((width, hid), BF16),
            jax.ShapeDtypeStruct((width, hid), BF16),
        ),
        in_specs=[vmem] * 2 + [anywhere] * 3,
        out_specs=(anywhere, vmem, anywhere, anywhere),
        scratch_shapes=[
            pltpu.VMEM((width, hid), BF16),
            pltpu.VMEM((width, hid), BF16),
            pltpu.VMEM((slots, hid), BF16),
            pltpu.VMEM((slots, hid), BF16),
            pltpu.VMEM((width, hid), BF16),
            pltpu.VMEM((width, hid), BF16),
            pltpu.VMEM((slots, count), BF16),
            pltpu.VMEM((slots, width), BF16),
            pltpu.VMEM((slots, width), BF16),
            pltpu.VMEM((slots, 2 * hid), BF16),
            pltpu.VMEM((ne // nd, nd, cap, 2 * hid), BF16),
            pltpu.VMEM((ne // nd, cap, 2 * hid), F32),
            pltpu.VMEM((slots, 2 * hid), BF16),
            pltpu.VMEM((slots, width), BF16),
            pltpu.VMEM((slots, width), BF16),
            pltpu.VMEM((ns, share, width), F32),
            pltpu.VMEM((ns, share, width), BF16),
            pltpu.VMEM((ns, share, width), BF16),
            pltpu.VMEM((ns, share, width), BF16),
            dma((3,)), dma((3,)), pltpu.SemaphoreType.REGULAR((ns // 2 - 1,)),
            dma((ne,)), dma((ne,)),
            dma((ne,)), dma((ne // nd, nd)),
            dma((ne // nd, 2)), dma((ne,)),
            dma((ne // nd, 2)), dma((ne, 2)),
            dma((ne // nd, nd)), dma((ne,)),
            dma((ne,)), dma((ne,)),
            dma((ns,)), dma((ns,)),
            dma((ns,)), dma((ns,)),
        ],
        compiler_params=pltpu.CompilerParams(collective_id=0, has_side_effects=True),
    )(tokens, expert_ids.T, w_gate[0], w_up[0], cotangent[0])
    n = len(outs)
    acted, grad_in, grad_gate, grad_up = pl.pallas_call(
        settle,
        out_shape=tuple(jax.ShapeDtypeStruct(o.shape, o.dtype) for o in outs),
        in_specs=[anywhere] * n,
        out_specs=(anywhere,) * n,
        scratch_shapes=[pltpu.VMEM(o.shape, o.dtype) for o in outs] + [dma((n, 4)), dma((n, 4))],
    )(*outs)
    return acted[None], grad_in.reshape(count, width), grad_gate[None], grad_up[None]


def solution(mesh):
    placed = (
        P("expert", "dp"),
        P("expert", None),
        P("expert", "dp", "section"),
        P("expert", "dp", "section"),
        P("expert", None, "section"),
    )
    return jax.shard_map(
        local,
        mesh=mesh,
        in_specs=placed,
        out_specs=(
            P("expert", None, "section"),
            P("expert", "dp"),
            P("expert", "dp", "section"),
            P("expert", "dp", "section"),
        ),
        check_vma=False,
    )
```

```python
import jax
import jax.numpy as jnp
from jax import lax
from jax.experimental import pallas as pl
from jax.experimental.pallas import tpu as pltpu
from jax.sharding import PartitionSpec as P

F32 = jnp.float32
BF16 = jnp.bfloat16
NN = (((1,), (0,)), ((), ()))
NT = (((1,), (1,)), ((), ()))
TN = (((0,), (0,)), ((), ()))


def dot(a, b, dims):
    return lax.dot_general(a, b, dims, preferred_element_type=F32)


def kernel(
    sizes,
    tok, ids, wg_hbm, wu_hbm, cot_hbm,
    acted_hbm, grad_in, gate_hbm, up_hbm,
    wg, wu, cot, acted, grad_gate, grad_up,
    pick, x_out, x_all, pre_out, pre_in, pre_own, parts,
    back_out, home, whole, z_out, z_in, z_all,
    in_sem, out_sem, known,
    x_ss, x_rs, p_ss, p_rs, a_ss, a_rs, f_ss, f_rs, o_ss, o_rs, h_ss, h_rs, zr_ss, zr_rs, za_ss, za_rs,
):
    ns, ne, nd = sizes
    s, e, d = lax.axis_index("section"), lax.axis_index("expert"), lax.axis_index("dp")
    cap = x_all.shape[0] // ne
    hid = wg.shape[1]
    per = ne // nd
    y, c = e // 2, e % 2
    ny = ne // 2

    def rows(g):
        return pl.ds(pl.multiple_of(g * cap, cap), cap)

    def expert_peer(k):
        return ((y + k // 2) % ny) * 2 + (c + k) % 2

    def send(src, dst, ss, rs, axis, peer):
        return pltpu.make_async_remote_copy(
            src_ref=src, dst_ref=dst, send_sem=ss, recv_sem=rs,
            device_id={axis: peer}, device_id_type=pl.DeviceIdType.MESH,
        )

    barrier = pltpu.get_barrier_semaphore()
    rounds = ns // 2 - 1
    greeted = (("section", s, ns, (1, ns - 1)), ("expert", e, ne, range(1, ne)), ("dp", d, nd, range(1, nd)))
    for axis, me, n, offsets in greeted:
        for k in offsets:
            pl.semaphore_signal(
                barrier, inc=1, device_id={axis: (me + k) % n},
                device_id_type=pl.DeviceIdType.MESH,
            )

    loads = [
        pltpu.make_async_copy(src, dst, in_sem.at[i])
        for i, (src, dst) in enumerate(((wg_hbm, wg), (wu_hbm, wu), (cot_hbm, cot)))
    ]
    for copy in loads:
        copy.start()

    count = tok.shape[0]
    named = lax.broadcasted_iota(jnp.int32, (ne, count), 0)
    member = (named == ids[0:1, :]) | (named == ids[1:2, :])
    before = lax.broadcasted_iota(jnp.int32, (count, count), 0) < lax.broadcasted_iota(
        jnp.int32, (count, count), 1
    )
    rank = dot(
        jnp.where(member, 1.0, 0.0).astype(BF16), jnp.where(before, 1.0, 0.0).astype(BF16), NN
    ).astype(jnp.int32)
    rank = jnp.where(member, rank, -1)
    at = lax.broadcasted_iota(jnp.int32, (cap, count), 0)
    for g in range(ne):
        pick[g * cap : (g + 1) * cap, :] = jnp.where(at == rank[g : g + 1, :], 1.0, 0.0).astype(
            BF16
        )

    def build(g):
        x_out[rows(g), :] = dot(pick[rows(g), :], tok[...], NN).astype(BF16)

    def x_copy(peer, slot):
        return send(
            x_out.at[rows(peer)], x_all.at[rows(slot)], x_ss.at[peer], x_rs.at[slot],
            "expert", peer,
        )

    near, two_away = (2, 3, 6, 7, 1), (4, 5)
    build(expert_peer(near[0]))
    pl.semaphore_wait(barrier, sum(len(g[3]) for g in greeted))
    for n, k in enumerate(near):
        if n:
            build(expert_peer(k))
        x_copy(expert_peer(k), e).start()
    x_all[rows(e), :] = dot(pick[rows(e), :], tok[...], NN).astype(BF16)
    for k in two_away:
        build(expert_peer(k))

    def spread(t):
        @pl.when((t > 0) & (t <= rounds))
        def _():
            pl.semaphore_wait(known.at[t - 1], 2)

        @pl.when(t < rounds)
        def _():
            for k in (1, ns - 1):
                pl.semaphore_signal(
                    known.at[t], inc=1, device_id={"section": (s + k) % ns},
                    device_id_type=pl.DeviceIdType.MESH,
                )

    def p_copy(g):
        i = g // nd
        return send(
            pre_out.at[rows(g)], pre_in.at[i, d], p_ss.at[g], p_rs.at[i, d], "dp", g % nd
        )

    for copy in loads[:2]:
        copy.wait()

    def forward(t, _):
        spread(t)
        k = jnp.where(
            t < 2, t, jnp.where(t < 4, 4 * (y % 2) + t, jnp.where(t < 6, 2 - 4 * (y % 2) + t, t - 2))
        )
        g = expert_peer(k)

        @pl.when(t > 0)
        def _():
            x_copy(g, g).wait_recv()

        x = x_all[rows(g), :]
        pg = dot(x, wg[...], NN)
        pu = dot(x, wu[...], NN)

        @pl.when(g % nd == d)
        def _():
            pre_own[g // nd, :, :hid] = pg
            pre_own[g // nd, :, hid:] = pu

        @pl.when(g % nd != d)
        def _():
            pre_out[rows(g), :hid] = pg.astype(BF16)
            pre_out[rows(g), hid:] = pu.astype(BF16)

        @pl.when(t == ne // 2)
        def _():
            for k in range(1, nd):
                p_copy(first * nd + (d + k) % nd).wait_send()

        @pl.when(g % nd != d)
        def _():
            p_copy(g).start()

        return 0

    first = y // (ny // per)

    lax.fori_loop(0, 2, forward, 0)
    for k in near:
        x_copy(expert_peer(k), e).wait_send()
    for k in two_away:
        x_copy(expert_peer(k), e).start()
    lax.fori_loop(2, ne, forward, 0)

    right, left = (d + 1) % nd, (d + nd - 1) % nd

    def a_copy(side, g):
        return send(
            parts.at[rows(g)], parts.at[rows(g)], a_ss.at[g // nd, side], a_rs.at[g],
            "dp", left if side else right,
        )

    def f_copy(side, g):
        part = pl.ds(pl.multiple_of(g * cap + side * (cap // 2), cap // 2), cap // 2)
        return send(
            parts.at[part], parts.at[part], f_ss.at[g // nd, side], f_rs.at[g, side],
            "dp", left if side else right,
        )

    def o_copy(peer, g):
        return send(
            acted.at[rows(g)], acted.at[rows(g)], o_ss.at[g // nd, peer], o_rs.at[g], "dp", peer
        )

    loads[2].wait()

    def owned(i):
        total = pre_own[i]
        for k in range(1, nd):
            src = (d + k) % nd
            send(
                pre_out.at[rows(0)], pre_in.at[i, src], p_ss.at[0], p_rs.at[i, src], "dp", src
            ).wait_recv()
            total = total + pre_in[i, src].astype(F32)
        g = i * nd + d
        pre_gate, pre_up = total[:, :hid], total[:, hid:]
        cf = cot[rows(g), :].astype(F32)
        sig = jax.nn.sigmoid(pre_gate)
        silu = pre_gate * sig
        gp = cf * pre_up * sig * (1.0 + pre_gate * (1.0 - sig))
        parts[rows(g), :hid] = gp.astype(BF16)
        parts[rows(g), hid:] = (cf * silu).astype(BF16)
        acted[rows(g), :] = (silu * pre_up).astype(BF16)
        for side in range(2):
            a_copy(side, g).start()

    def h_copy(g):
        return send(back_out.at[rows(g)], home.at[rows(e)], h_ss.at[g], h_rs.at[e], "expert", g)

    def arrive(i, k):
        g = i * nd + (d + k) % nd
        if k == 1:
            a_copy(0, g).wait_recv()
            f_copy(1, g).start()
        elif k == nd - 1:
            a_copy(0, g).wait_recv()
            f_copy(0, g).start()
        elif k > 0:
            f_copy(0, g).wait_recv()
            f_copy(1, g).wait_recv()

    def backward(i, k):
        g = i * nd + (d + k) % nd
        back = dot(parts[rows(g), :hid], wg[...], NT) + dot(parts[rows(g), hid:], wu[...], NT)

        @pl.when(g == e)
        def _():
            home[rows(g), :] = back.astype(BF16)

        @pl.when(g != e)
        def _():
            back_out[rows(g), :] = back.astype(BF16)
            h_copy(g).start()

    def mine(t, _):
        i = (first + t) % per
        owned(i)
        backward(i, 0)
        return 0

    def beside(t, _):
        i = (first + t) % per
        arrive(i, 1)
        arrive(i, 3)
        backward(i, 1)
        backward(i, 3)
        return 0

    def opposite(t, _):
        arrive((first + t) % per, 2)
        backward((first + t) % per, 2)
        return 0

    for step in (mine, beside, opposite):
        lax.fori_loop(0, per, step, 0)
    for i in range(per):
        for k in range(1, nd):
            o_copy((d + k) % nd, i * nd + d).start()

    for k in range(1, ne):
        src = expert_peer(k)
        send(
            back_out.at[rows(src)], home.at[rows(src)], h_ss.at[src], h_rs.at[src], "expert", src
        ).wait_recv()
    part = dot(pick[...], home[...], TN).reshape(whole.shape)
    whole[...] = part
    z_out[...] = part.astype(BF16)

    far = [k for j in range(ns // 2, 0, -1) for k in dict.fromkeys((j, ns - j))]

    def zr_copy(peer, slot):
        return send(
            z_out.at[peer], z_in.at[slot], zr_ss.at[peer], zr_rs.at[slot], "section", peer
        )

    def za_copy(peer, slot):
        return send(
            z_all.at[slot], z_all.at[slot], za_ss.at[peer], za_rs.at[slot], "section", peer
        )

    for k in far:
        zr_copy((s + k) % ns, s).start()

    tile = 128

    def weights(i, _):
        at = pl.ds(pl.multiple_of(i * tile, tile), tile)
        x = x_all[:, at]
        grad_gate[at, :] = dot(x, parts[:, :hid], TN).astype(BF16)
        grad_up[at, :] = dot(x, parts[:, hid:], TN).astype(BF16)
        return 0

    lax.fori_loop(0, wg.shape[0] // tile, weights, 0)
    stores = [
        pltpu.make_async_copy(src, dst, out_sem.at[i])
        for i, (src, dst) in enumerate(
            ((grad_gate, gate_hbm), (grad_up, up_hbm), (acted, acted_hbm))
        )
    ]
    for copy in stores[:2]:
        copy.start()

    total = whole[s]
    for k in reversed(far):
        src = (s + k) % ns
        zr_copy(src, src).wait_recv()
        total = total + z_in[src].astype(F32)
    z_all[s] = total.astype(BF16)
    for k in far:
        za_copy((s + k) % ns, s).start()
    for i in range(per):
        for k in range(1, nd):
            src = (d + k) % nd
            o_copy(src, i * nd + src).wait_recv()
    stores[2].start()
    for k in reversed(far):
        src = (s + k) % ns
        za_copy(src, src).wait_recv()
    grad_in[...] = z_all[...]

    for k in two_away:
        x_copy(expert_peer(k), e).wait_send()
    for k in range(1, ne):
        h_copy(expert_peer(k)).wait_send()
    for k in range(1, nd):
        p_copy((first + 1) % per * nd + (d + k) % nd).wait_send()
    for i in range(per):
        for k in range(1, nd):
            o_copy((d + k) % nd, i * nd + d).wait_send()
        for side in range(2):
            a_copy(side, i * nd + d).wait_send()
            f_copy(side, i * nd + d).wait_send()
    for k in far:
        zr_copy((s + k) % ns, s).wait_send()
        za_copy((s + k) % ns, s).wait_send()
    for copy in stores:
        copy.wait()


def settle(*refs):
    n = (len(refs) - 2) // 3
    src, dst, held, (in_sem, out_sem) = refs[:n], refs[n : 2 * n], refs[2 * n : 3 * n], refs[3 * n :]
    pieces = in_sem.shape[1]
    reads, writes = [], []
    for i in range(n):
        size = src[i].shape[0] // pieces
        for p in range(pieces):
            at = pl.ds(p * size, size)
            reads.append(
                pltpu.make_async_copy(src[i].at[at], held[i].at[at], in_sem.at[i, p])
            )
            writes.append(
                pltpu.make_async_copy(held[i].at[at], dst[i].at[at], out_sem.at[i, p])
            )
    for copy in reads:
        copy.start()
    for read, write in zip(reads, writes):
        read.wait()
        write.start()
    for copy in writes:
        copy.wait()


def local(tokens, expert_ids, w_gate, w_up, cotangent):
    count, width = tokens.shape
    ns, ne, nd = (lax.axis_size(a) for a in ("section", "expert", "dp"))
    hid = w_gate.shape[2]
    slots = cotangent.shape[1]
    cap = slots // ne
    vmem = pl.BlockSpec(memory_space=pltpu.VMEM)
    dma = pltpu.SemaphoreType.DMA
    share = count // ns
    anywhere = pl.BlockSpec(memory_space=pl.ANY)
    outs = pl.pallas_call(
        lambda *refs: kernel((ns, ne, nd), *refs),
        out_shape=(
            jax.ShapeDtypeStruct((slots, hid), BF16),
            jax.ShapeDtypeStruct((ns, share, width), BF16),
            jax.ShapeDtypeStruct((width, hid), BF16),
            jax.ShapeDtypeStruct((width, hid), BF16),
        ),
        in_specs=[vmem] * 2 + [anywhere] * 3,
        out_specs=(anywhere, vmem, anywhere, anywhere),
        scratch_shapes=[
            pltpu.VMEM((width, hid), BF16),
            pltpu.VMEM((width, hid), BF16),
            pltpu.VMEM((slots, hid), BF16),
            pltpu.VMEM((slots, hid), BF16),
            pltpu.VMEM((width, hid), BF16),
            pltpu.VMEM((width, hid), BF16),
            pltpu.VMEM((slots, count), BF16),
            pltpu.VMEM((slots, width), BF16),
            pltpu.VMEM((slots, width), BF16),
            pltpu.VMEM((slots, 2 * hid), BF16),
            pltpu.VMEM((ne // nd, nd, cap, 2 * hid), BF16),
            pltpu.VMEM((ne // nd, cap, 2 * hid), F32),
            pltpu.VMEM((slots, 2 * hid), BF16),
            pltpu.VMEM((slots, width), BF16),
            pltpu.VMEM((slots, width), BF16),
            pltpu.VMEM((ns, share, width), F32),
            pltpu.VMEM((ns, share, width), BF16),
            pltpu.VMEM((ns, share, width), BF16),
            pltpu.VMEM((ns, share, width), BF16),
            dma((3,)), dma((3,)), pltpu.SemaphoreType.REGULAR((ns // 2 - 1,)),
            dma((ne,)), dma((ne,)),
            dma((ne,)), dma((ne // nd, nd)),
            dma((ne // nd, 2)), dma((ne,)),
            dma((ne // nd, 2)), dma((ne, 2)),
            dma((ne // nd, nd)), dma((ne,)),
            dma((ne,)), dma((ne,)),
            dma((ns,)), dma((ns,)),
            dma((ns,)), dma((ns,)),
        ],
        compiler_params=pltpu.CompilerParams(collective_id=0, has_side_effects=True),
    )(tokens, expert_ids.T, w_gate[0], w_up[0], cotangent[0])
    n = len(outs)
    acted, grad_in, grad_gate, grad_up = pl.pallas_call(
        settle,
        out_shape=tuple(jax.ShapeDtypeStruct(o.shape, o.dtype) for o in outs),
        in_specs=[anywhere] * n,
        out_specs=(anywhere,) * n,
        scratch_shapes=[pltpu.VMEM(o.shape, o.dtype) for o in outs] + [dma((n, 4)), dma((n, 4))],
    )(*outs)
    return acted[None], grad_in.reshape(count, width), grad_gate[None], grad_up[None]


def solution(mesh):
    placed = (
        P("expert", "dp"),
        P("expert", None),
        P("expert", "dp", "section"),
        P("expert", "dp", "section"),
        P("expert", None, "section"),
    )
    return jax.shard_map(
        local,
        mesh=mesh,
        in_specs=placed,
        out_specs=(
            P("expert", None, "section"),
            P("expert", "dp"),
            P("expert", "dp", "section"),
            P("expert", "dp", "section"),
        ),
        check_vma=False,
    )
```
